32 devices in a mesh: row: 8 (over y, x, core), col: 4 (over z).
Axes of the slice: x: 2, y: 2, z: 4, core: 2. Of those that a mesh axis runs over, the one named last changes fastest.
Arguments:
- node_features: bfloat16 [8192, 128], P(('row', 'col')), may hold values from -6 to 6
- tile_values: bfloat16 [8, 4, 384, 128, 128], P('row', 'col'), may hold values from -0.078125 to 0.078125
- tile_rows: int32 [8, 4, 384], P('row', 'col'), may hold values from 0 to 7
- tile_cols: int32 [8, 4, 384], P('row', 'col'), may hold values from 0 to 15
- tile_count: int32 [8, 4], P('row', 'col'), may hold values from 48 to 384, as said below
- labels: int32 [8192], P(('row', 'col')), may hold values from 0 to 46
- train_mask: int32 [8192], P(('row', 'col')), may hold values from 0 to 1, as said below
- hidden_weight: bfloat16 [128, 256], replicated, may hold values from -0.5 to 0.5
- hidden_bias: float32 [256], replicated, may hold values from -3 to 3
- class_weight: bfloat16 [256, 47], replicated, may hold values from -3.59375 to 3.59375
- class_bias: float32 [47], replicated, may hold values from -4 to 4
Outputs:
- hidden: bfloat16 [8192, 256], P(('row', 'col'))
- logits: float32 [47, 8192], P(None, ('row', 'col'))
- mean_loss: float32 [], replicated
- hidden_weight_grad: float32 [128, 256], replicated
- hidden_bias_grad: float32 [256], replicated
- class_weight_grad: float32 [256, 47], replicated
- class_bias_grad: float32 [47], replicated
The draws below stay inside these ranges and needn't reach their ends.
Inputs may be any that keep to these rules, and one draw needn't show every extreme that they name: Slots s >= tile_count of a block are not part of it; some block has all 384 slots live. `train_mask`: at least one node is a training node.
All inputs are finite; a program needn't handle non-finite values.
Results may differ from the reference program's by a relative error of at most 0.025.
Values may be sent and summed in bfloat16 or wider, within the bound.
No kernel may reach another device: no remote copies, remote signals or barrier semaphores. Data moves between devices by JAX's collectives and lax.ppermute only.
A program may use at most 128 MiB of HBM per device.

```python
import jax
import jax.numpy as jnp
from jax import lax

F_IN = 128
HIDDEN_SIZE = 256
CLASSES = 47
TILE = 128
NODES_DEV = 256
TILES_DEV = 384
NODES = 8192
N_ROW = 8
N_COL = 4


def draw_tile_count(key, part):
    lowest = max(1, TILES_DEV // 8)
    highest = max(TILES_DEV // 2 + 1, lowest + 1)
    positions = N_ROW * N_COL
    counts = jax.random.randint(key, (positions,), lowest, highest)
    chosen = jax.random.randint(jax.random.fold_in(key, 7), (), 0, positions)
    counts = jnp.where(jnp.arange(positions) == chosen, TILES_DEV, counts)
    return counts.reshape(N_ROW, N_COL).astype(jnp.int32)


def draw_train_mask(key, part):
    slices = jnp.arange(NODES) // NODES_DEV
    positions = N_ROW * N_COL
    chance = 150 + 300 * slices // max(positions - 1, 1)
    rolled = jax.random.randint(key, (NODES,), 0, 1000)
    marked = (rolled < chance).astype(jnp.int32)
    return marked.at[0].set(1).astype(jnp.int32)


def place_ends(result, stream_key, least, high):
    place = [jax.random.randint(jax.random.fold_in(stream_key, axis), (), 0, length) for axis, length in enumerate(result.shape)]
    longest = result.shape.index(max(result.shape))
    neighbour = place[:longest] + [(place[longest] + 1) % result.shape[longest]] + place[longest + 1:]
    return result.at[tuple(place)].set(least).at[tuple(neighbour)].set(high)


def steps_of(own_key, extent, cuts, low, largest):
    level = 1.0
    for dim, shards_of in cuts:
        draws = jax.random.uniform(jax.random.fold_in(jax.random.fold_in(own_key, 6), dim), (shards_of,), jnp.float32, low / len(cuts), largest / len(cuts))
        level = level * jnp.repeat(jnp.exp(draws), extent[dim] // shards_of).reshape((-1,) + (1,) * (len(extent) - 1 - dim))
    return level


def normal_values(key, extent, spread, bound, split=(), kind=jnp.bfloat16):
    array = spread * jax.random.normal(key, extent, jnp.float32)
    if split:
        array = array * steps_of(key, extent, split, -0.22, 0.18)
    return jnp.clip(array, -bound, bound).astype(kind)


def setup_inputs(seed: int = 0) -> dict:
    key_list = jax.random.split(jax.random.key(seed), 12)
    return {
        "node_features": normal_values(key_list[0], (NODES, F_IN), 1.0, 6.0, ((0, 32),)),
        "tile_values": normal_values(key_list[1], (N_ROW, N_COL, TILES_DEV, TILE, TILE), (TILE * TILE * TILES_DEV // (N_COL * NODES_DEV)) ** -0.5, 0.078125, ((0, 8), (1, 4))),
        "tile_rows": place_ends(jax.random.randint(key_list[2], (N_ROW, N_COL, TILES_DEV), 0, N_COL * NODES_DEV // TILE), jax.random.fold_in(key_list[2], 1), 0, (N_COL * NODES_DEV // TILE) - 1).astype(jnp.int32),
        "tile_cols": place_ends(jax.random.randint(key_list[3], (N_ROW, N_COL, TILES_DEV), 0, N_ROW * NODES_DEV // TILE), jax.random.fold_in(key_list[3], 1), 0, (N_ROW * NODES_DEV // TILE) - 1).astype(jnp.int32),
        "tile_count": draw_tile_count(jax.random.fold_in(key_list[11], 71), 0),
        "labels": place_ends(jax.random.randint(key_list[5], (NODES,), 0, CLASSES), jax.random.fold_in(key_list[5], 1), 0, CLASSES - 1).astype(jnp.int32),
        "train_mask": draw_train_mask(jax.random.fold_in(key_list[11], 71), 0),
        "hidden_weight": normal_values(key_list[7], (F_IN, HIDDEN_SIZE), F_IN ** -0.5, 0.5),
        "hidden_bias": normal_values(key_list[8], (HIDDEN_SIZE,), 0.5, 3.0, (), jnp.float32),
        "class_weight": normal_values(key_list[9], (HIDDEN_SIZE, CLASSES), 0.6, 3.59375),
        "class_bias": normal_values(key_list[10], (CLASSES,), 1.0, 4.0, (), jnp.float32),
    }


def block_product(values, tile_rows, tile_cols, tile_total, source, out_tiles, transpose):
    feature_width = source.shape[1]
    tiled = source.reshape(-1, TILE, feature_width).astype(jnp.float32)
    if transpose:
        pieces = tiled[tile_rows]
        product = jnp.einsum("gji,gjf->gif", values.astype(jnp.float32), pieces, precision=lax.Precision.HIGHEST)
        target = tile_cols
    else:
        pieces = tiled[tile_cols]
        product = jnp.einsum("gij,gjf->gif", values.astype(jnp.float32), pieces, precision=lax.Precision.HIGHEST)
        target = tile_rows
    live_slots = (jnp.arange(TILES_DEV) < tile_total).astype(jnp.float32)
    product = product * live_slots[:, None, None]
    summed = jax.ops.segment_sum(product, target, num_segments=out_tiles)
    return summed.reshape(out_tiles * TILE, feature_width)


def rounded(term):
    return lax.optimization_barrier(term.astype(jnp.bfloat16)).astype(jnp.float32)


def aggregate(source, tile_values, tile_rows, tile_cols, tile_count, round_terms):
    feature_width = source.shape[1]
    grid = source.reshape(N_ROW, N_COL, NODES_DEV, feature_width)

    def one_row(row_index):
        def add_col(total, col_index):
            column_block = grid[:, col_index].reshape(N_ROW * NODES_DEV, feature_width)
            term = block_product(tile_values[row_index, col_index], tile_rows[row_index, col_index], tile_cols[row_index, col_index], tile_count[row_index, col_index], column_block, N_COL * NODES_DEV // TILE, False)
            if round_terms:
                term = rounded(term)
            return total + term, None

        start = jnp.zeros((N_COL * NODES_DEV, feature_width), jnp.float32)
        total, _ = lax.scan(add_col, start, jnp.arange(N_COL))
        return total

    return lax.map(one_row, jnp.arange(N_ROW)).reshape(NODES, feature_width)


def aggregate_back(source, tile_values, tile_rows, tile_cols, tile_count):
    feature_width = source.shape[1]
    grid = source.reshape(N_ROW, N_COL * NODES_DEV, feature_width)

    def one_col(col_index):
        def add_row(total, row_index):
            term = block_product(tile_values[row_index, col_index], tile_rows[row_index, col_index], tile_cols[row_index, col_index], tile_count[row_index, col_index], grid[row_index], N_ROW * NODES_DEV // TILE, True)
            return total + term, None

        start = jnp.zeros((N_ROW * NODES_DEV, feature_width), jnp.float32)
        total, _ = lax.scan(add_row, start, jnp.arange(N_ROW))
        return total

    columns = lax.map(one_col, jnp.arange(N_COL))
    return columns.reshape(N_COL, N_ROW, NODES_DEV, feature_width).transpose(1, 0, 2, 3).reshape(NODES, feature_width)


def reference(node_features, tile_values, tile_rows, tile_cols, tile_count, labels, train_mask, hidden_weight, hidden_bias, class_weight, class_bias):
    first_agg = aggregate(node_features, tile_values, tile_rows, tile_cols, tile_count, True).astype(jnp.bfloat16)
    hidden_pre = jnp.dot(first_agg, hidden_weight, preferred_element_type=jnp.float32) + hidden_bias
    hidden = jax.nn.silu(hidden_pre).astype(jnp.bfloat16)
    second_agg = aggregate(hidden, tile_values, tile_rows, tile_cols, tile_count, False)
    class_weight_wide = class_weight.astype(jnp.float32)
    logits = jnp.einsum("hk,nh->kn", class_weight_wide, second_agg, precision=lax.Precision.HIGHEST) + class_bias[:, None]
    top = jnp.max(logits, axis=0)
    log_total = top + jnp.log(jnp.sum(jnp.exp(logits - top[None, :]), axis=0))
    onehot = (jnp.arange(CLASSES)[:, None] == labels[None, :]).astype(jnp.float32)
    cross_entropy = log_total - jnp.sum(onehot * logits, axis=0)
    weights = train_mask.astype(jnp.float32)
    count = jnp.sum(weights)
    mean_loss = jnp.sum(weights * cross_entropy) / count
    class_grad = (jnp.exp(logits - log_total[None, :]) - onehot) * (weights / count)[None, :]
    class_weight_grad = jnp.einsum("nh,kn->hk", second_agg, class_grad, precision=lax.Precision.HIGHEST)
    class_bias_grad = jnp.sum(class_grad, axis=1)
    agg_grad = jnp.einsum("kn,hk->nh", class_grad, class_weight_wide, precision=lax.Precision.HIGHEST)
    hidden_grad = aggregate_back(agg_grad, tile_values, tile_rows, tile_cols, tile_count)
    sigma = jax.nn.sigmoid(hidden_pre)
    pre_grad = hidden_grad * sigma * (1.0 + hidden_pre * (1.0 - sigma))
    hidden_weight_grad = jnp.einsum("nf,nh->fh", first_agg.astype(jnp.float32), pre_grad, precision=lax.Precision.HIGHEST)
    hidden_bias_grad = jnp.sum(pre_grad, axis=0)
    return (hidden, logits, mean_loss, hidden_weight_grad, hidden_bias_grad, class_weight_grad, class_bias_grad)
```

```python
import functools
import math

import jax
import jax.numpy as jnp
from jax import lax
from jax.experimental import pallas as pl
from jax.experimental.pallas import tpu as pltpu
from jax.sharding import PartitionSpec as P

TILE = 128
MASK_CODE = 128
LIMIT = 48 * 1024 * 1024
WIRE = jnp.float32
f32 = jnp.float32
bf16 = jnp.bfloat16


VMEM = pl.BlockSpec(memory_space=pltpu.VMEM)
SMEM = pl.BlockSpec(memory_space=pltpu.SMEM)
ANY = pl.BlockSpec(memory_space=pl.ANY)


def params(limit=LIMIT):
    return pltpu.CompilerParams(vmem_limit_bytes=limit)


def cost(flops, moved, transcendentals=0):
    return pl.CostEstimate(flops=flops, bytes_accessed=moved, transcendentals=transcendentals)


def dot(a, b, dims=((1,), (0,))):
    return lax.dot_general(a, b, (dims, ((), ())), preferred_element_type=f32)


def halves(value):
    high = value.astype(bf16)
    return high, (value - high.astype(f32)).astype(bf16)


def densify_kernel(group, depth, banks, tile_rows, tile_cols, rows, cols, count, values, out, ring, *rest):
    totals, sem = rest[:banks], rest[banks]
    live = count[0, 0]
    groups = (live + group - 1) // group
    spare = tile_rows * tile_cols

    def copy(index, slot):
        return pltpu.make_async_copy(
            values.at[pl.ds(index * group, group)], ring.at[slot], sem.at[slot]
        )

    for slot in range(depth):
        @pl.when(slot < groups)
        def _():
            copy(slot, slot).start()

    for total in totals:
        @pl.loop(0, spare)
        def _(place):
            total[place] = jnp.zeros((TILE, TILE), f32)

    @pl.loop(0, groups)
    def _(index):
        slot = lax.rem(index, depth)
        copy(index, slot).wait()
        for k in range(group):
            item = index * group + k
            place = rows[0, item] * tile_cols + cols[0, item]
            place = jnp.where(item < live, place, spare)
            total = totals[k % banks]
            total[place] = total[place] + ring[slot, k].astype(f32)

        @pl.when(index + depth < groups)
        def _():
            copy(index + depth, slot).start()

    for tile_row in range(tile_rows):
        @pl.loop(0, tile_cols)
        def _(tile_col):
            place = tile_row * tile_cols + tile_col
            summed = functools.reduce(lambda a, b: a + b, [total[place] for total in totals])
            lanes = pl.ds(pl.multiple_of(tile_col * TILE, TILE), TILE)
            out[pl.ds(tile_row * TILE, TILE), lanes] = summed.astype(bf16)


def densify(values, rows, cols, count, tile_rows, tile_cols):
    slots = values.shape[0]
    group = math.gcd(slots, 16)
    places = tile_rows * tile_cols
    banks = 2 if places <= 128 else 1
    depth = min(slots // group, 8)
    return pl.pallas_call(
        functools.partial(densify_kernel, group, depth, banks, tile_rows, tile_cols),
        out_shape=jax.ShapeDtypeStruct((tile_rows * TILE, tile_cols * TILE), bf16),
        in_specs=[SMEM, SMEM, SMEM, ANY],
        out_specs=VMEM,
        scratch_shapes=[pltpu.VMEM((depth, group, TILE, TILE), bf16)]
        + [pltpu.VMEM((places + 1, TILE, TILE), f32) for _ in range(banks)]
        + [pltpu.SemaphoreType.DMA((depth,))],
        compiler_params=params(58 * 1024 * 1024 if banks == 1 else LIMIT),
        cost_estimate=cost(slots * TILE * TILE, slots * TILE * TILE * 2),
        name="densify",
    )(rows, cols, count, values)


def first_kernel(n_row, n_col, ids, dense, *refs):
    pieces, outs, stacked = refs[:n_row], refs[n_row : n_row + n_col], refs[n_row + n_col]
    nodes = pieces[0].shape[0]
    row, col = ids[0], ids[1]
    for k in range(n_row):
        place = pl.multiple_of((row ^ k) * nodes, nodes)
        stacked[pl.ds(place, nodes), :] = pieces[k][...]
    for k in range(n_col):
        place = pl.multiple_of((col ^ k) * nodes, nodes)
        outs[k][...] = dot(dense[pl.ds(place, nodes), :], stacked[...]).astype(bf16)


def first_terms(ids, dense, pieces, n_col):
    nodes, width = pieces[0].shape
    n_row = len(pieces)
    return pl.pallas_call(
        functools.partial(first_kernel, n_row, n_col),
        out_shape=[jax.ShapeDtypeStruct((nodes, width), bf16)] * n_col,
        in_specs=[SMEM, VMEM] + [VMEM] * n_row,
        out_specs=[VMEM] * n_col,
        scratch_shapes=[pltpu.VMEM((n_row * nodes, width), bf16)],
        compiler_params=params(),
        cost_estimate=cost(2 * dense.size * width, dense.size * 2),
        name="first_terms",
    )(ids, dense, *pieces)


def hidden_kernel(n_row, n_col, ids, dense, weight, bias, class_weight, code, *refs):
    pieces = refs[:n_row]
    hidden_out, column_out, term_out, stacked = refs[n_row:]
    nodes = pieces[0].shape[0]
    row, col = ids[0], ids[1]
    for k in range(n_row):
        pre = dot(pieces[k][...], weight[...]) + bias[...]
        hidden = (pre * (1.0 / (1.0 + jnp.exp(-pre)))).astype(bf16)
        place = pl.multiple_of((row ^ k) * nodes, nodes)
        column_out[pl.ds(place, nodes), :] = hidden
        if k == 0:
            hidden_out[...] = hidden
        high, low = halves(dot(hidden, class_weight[...]))
        stacked[pl.ds(place, nodes), :] = jnp.concatenate([high, low], axis=1)
    both = dot(dense[...], stacked[...])
    lanes = both.shape[1] // 2
    term = (both[:, :lanes] + both[:, lanes:]).T[: term_out.shape[0]]
    slice_of = lax.broadcasted_iota(jnp.int32, term.shape, 1) // nodes
    line = lax.broadcasted_iota(jnp.int32, term.shape, 0)
    codes = jnp.where(slice_of == col, jnp.concatenate([code[...]] * n_col, axis=1), 0.0)
    term_out[...] = jnp.where(line == term.shape[0] - 1, codes, term).astype(bf16)


def hidden_terms(ids, dense, weight, bias, class_weight, code, pieces, n_col, lines):
    nodes = pieces[0].shape[0]
    n_row = len(pieces)
    width = weight.shape[1]
    lanes = class_weight.shape[1]
    column = n_row * nodes
    return pl.pallas_call(
        functools.partial(hidden_kernel, n_row, n_col),
        out_shape=[
            jax.ShapeDtypeStruct((nodes, width), bf16),
            jax.ShapeDtypeStruct((column, width), bf16),
            jax.ShapeDtypeStruct((lines, n_col * nodes), bf16),
        ],
        in_specs=[SMEM] + [VMEM] * (5 + n_row),
        out_specs=[VMEM] * 3,
        scratch_shapes=[pltpu.VMEM((column, 2 * lanes), bf16)],
        compiler_params=params(),
        cost_estimate=cost(4 * dense.size * lanes, dense.size * 2, column * width * 2),
        name="hidden_terms",
    )(ids, dense, weight, bias, class_weight, code, *pieces)


def slope_kernel(n_row, ids, weight, bias, *refs):
    pieces = refs[:n_row]
    slope_out, turned_out = refs[n_row:]
    nodes = pieces[0].shape[0]
    row = ids[0]
    for k in range(n_row):
        pre = dot(pieces[k][...], weight[...]) + bias[...]
        sigma = 1.0 / (1.0 + jnp.exp(-pre))
        place = pl.multiple_of((row ^ k) * nodes, nodes)
        slope_out[pl.ds(place, nodes), :] = sigma * (1.0 + pre * (1.0 - sigma))
        turned_out[:, pl.ds(place, nodes)] = pieces[k][...].T


def slopes(ids, weight, bias, pieces):
    nodes, features = pieces[0].shape
    n_row = len(pieces)
    width = weight.shape[1]
    column = n_row * nodes
    return pl.pallas_call(
        functools.partial(slope_kernel, n_row),
        out_shape=[
            jax.ShapeDtypeStruct((column, width), f32),
            jax.ShapeDtypeStruct((features, column), bf16),
        ],
        in_specs=[SMEM] + [VMEM] * (2 + n_row),
        out_specs=[VMEM] * 2,
        compiler_params=params(),
        cost_estimate=cost(2 * column * features * width, column * width * 4, column * width * 2),
        name="slopes",
    )(ids, weight, bias, *pieces)


def tree_sum(parts):
    parts = [part.astype(f32) for part in parts]
    while len(parts) > 1:
        parts = [parts[k] + parts[k + 1] for k in range(0, len(parts), 2)]
    return parts[0]


def gradient_kernel(n_col, classes, ids, dense, column, slope, turned, class_weight_turned, class_bias, *refs):
    terms = refs[:n_col]
    logits_out, keep_out, send_out, scratch, packed = refs[n_col:]
    lines, nodes_row = terms[0].shape
    nodes = nodes_row // n_col
    features = turned.shape[0]
    width = column.shape[1]
    row, col = ids[0], ids[1]
    total = tree_sum([term[...] for term in terms])
    code = total[lines - 1 :, :]
    live = (code >= MASK_CODE).astype(f32)
    label = (code - MASK_CODE * live).astype(jnp.int32)
    line = lax.broadcasted_iota(jnp.int32, total.shape, 0)
    logits = jnp.where(line < classes, total + class_bias[...], -jnp.inf)
    scratch[...] = logits
    own = pl.ds(pl.multiple_of(col * nodes, nodes), nodes)
    logits_out[...] = scratch[:classes, own]
    top = jnp.max(logits, axis=0, keepdims=True)
    log_total = top + jnp.log(jnp.sum(jnp.exp(logits - top), axis=0, keepdims=True))
    chosen = line == label
    picked = jnp.sum(jnp.where(chosen, logits, 0.0), axis=0, keepdims=True)
    grad = (jnp.exp(logits - log_total) - chosen.astype(f32)) * live
    high, low = halves(grad)
    stacked = jnp.concatenate([high, low], axis=0)
    both = dot(stacked, dense[...])
    back = both[:lines] + both[lines:]
    back_high, back_low = halves(back)
    back_both = jnp.concatenate([back_high, back_low], axis=0)
    class_both = dot(back_both, column[...])
    packed[pl.ds(features, lines), :] = class_both[:lines] + class_both[lines:]
    hidden_grad = dot(back_both, class_weight_turned[...], ((0,), (0,)))
    pre_grad = hidden_grad * slope[...]
    pre_high, pre_low = halves(pre_grad)
    packed[pl.ds(0, features), :] = dot(turned[...], pre_high) + dot(turned[...], pre_low)
    packed[pl.ds(features + lines - 1, 1), :] = jnp.sum(pre_grad, axis=0, keepdims=True)
    here = (lax.broadcasted_iota(jnp.int32, (8, nodes_row), 1) // nodes == col).astype(f32)
    ours = here.astype(bf16)
    class_sum = dot(ours, high, ((1,), (1,))) + dot(ours, low, ((1,), (1,)))
    class_sum = jnp.concatenate([class_sum, jnp.zeros((8, width - lines), f32)], axis=1)
    loss = jnp.sum((log_total - picked) * live * here[:1])
    members = jnp.sum(live * here[:1])
    lane = lax.broadcasted_iota(jnp.int32, (8, width), 1)
    tail = jnp.where(lane == 0, loss, jnp.where(lane == 1, members, 0.0))
    packed[pl.ds(features + lines, 8), :] = class_sum
    packed[pl.ds(features + lines + 8, 8), :] = tail
    part = packed.shape[0] // 2
    core = row & 1
    keep_out[...] = packed[pl.ds(pl.multiple_of(core * part, 8), part), :]
    send_out[...] = packed[pl.ds(pl.multiple_of((1 - core) * part, 8), part), :]


def gradients(ids, dense, column, slope, turned, class_weight_turned, class_bias, terms, classes):
    n_col = len(terms)
    lines, nodes_row = terms[0].shape
    width = column.shape[1]
    packed = turned.shape[0] + lines + 16
    return pl.pallas_call(
        functools.partial(gradient_kernel, n_col, classes),
        out_shape=[
            jax.ShapeDtypeStruct((classes, nodes_row // n_col), f32),
            jax.ShapeDtypeStruct((packed // 2, width), f32),
            jax.ShapeDtypeStruct((packed // 2, width), f32),
        ],
        in_specs=[SMEM] + [VMEM] * (6 + n_col),
        out_specs=[VMEM] * 3,
        scratch_shapes=[
            pltpu.VMEM((lines, nodes_row), f32),
            pltpu.VMEM((packed, width), f32),
        ],
        compiler_params=params(),
        cost_estimate=cost(4 * dense.size * lines, dense.size * 2),
        name="gradients",
    )(ids, dense, column, slope, turned, class_weight_turned, class_bias, *terms)


def finish_kernel(features, lines, classes, ids, mine, other, loss_out, weight_out, bias_out, class_out, class_bias_out, packed):
    part = mine.shape[0]
    core = ids[0] & 1
    packed[pl.ds(pl.multiple_of(core * part, 8), part), :] = mine[...].astype(f32)
    packed[pl.ds(pl.multiple_of((1 - core) * part, 8), part), :] = other[...].astype(f32)
    tail = packed[pl.ds(features + lines + 8, 8), :]
    members = tail[:1, 1:2]
    loss_out[...] = tail[:1, :1] / members
    weight_out[...] = packed[pl.ds(0, features), :] / members
    bias_out[...] = packed[pl.ds(features + lines - 1, 1), :] / members
    class_out[...] = (packed[pl.ds(features, lines), :] / members).T[:, :classes]
    class_bias_out[...] = packed[pl.ds(features + lines, 1), :][:, :classes] / members


def finish(ids, mine, other, features, lines, classes):
    part, width = mine.shape
    return pl.pallas_call(
        functools.partial(finish_kernel, features, lines, classes),
        out_shape=[
            jax.ShapeDtypeStruct((1, 1), f32),
            jax.ShapeDtypeStruct((features, width), f32),
            jax.ShapeDtypeStruct((1, width), f32),
            jax.ShapeDtypeStruct((width, classes), f32),
            jax.ShapeDtypeStruct((1, classes), f32),
        ],
        in_specs=[SMEM, VMEM, VMEM],
        out_specs=[VMEM] * 5,
        scratch_shapes=[pltpu.VMEM((2 * part, width), f32)],
        compiler_params=params(),
        name="finish",
    )(ids, mine, other)


def swap(value, axis, mask):
    size = lax.axis_size(axis)
    return lax.ppermute(value, axis, [(k, k ^ mask) for k in range(size)])


def gather_row(value):
    size = lax.axis_size("row")
    even = [value] + [swap(value, "row", k) for k in range(2, size, 2)]
    odd = [swap(piece, "row", 1) for piece in even]
    return [piece for pair in zip(even, odd) for piece in pair]


def sum_over(value, axis, low, high):
    while low < high:
        step = min(2, high - low)
        parts = [value.astype(WIRE)]
        parts += [swap(parts[0], axis, k << low) for k in range(1, 1 << step)]
        value = tree_sum(parts)
        low += step
    return value


def on_device(
    node_features,
    tile_values,
    tile_rows,
    tile_cols,
    tile_count,
    labels,
    train_mask,
    hidden_weight,
    hidden_bias,
    class_weight,
    class_bias,
):
    nodes, features = node_features.shape
    classes = class_weight.shape[1]
    n_row, n_col = lax.axis_size("row"), lax.axis_size("col")
    row_bits, col_bits = n_row.bit_length() - 1, n_col.bit_length() - 1
    lines = (classes // 16 + 1) * 16
    ids = jnp.stack([lax.axis_index("row"), lax.axis_index("col")]).astype(jnp.int32)
    code = (labels + MASK_CODE * train_mask).astype(f32)[None, :]
    bias = hidden_bias[None, :]
    class_lanes = jnp.pad(class_weight, ((0, 0), (0, 128 - classes)))
    class_turned = jnp.pad(class_weight.T, ((0, lines - classes), (0, 0)))
    class_turned = jnp.concatenate([class_turned, class_turned], axis=0)
    class_bias_lines = jnp.pad(class_bias, (0, lines - classes))[:, None]

    sources = gather_row(node_features)
    dense = densify(
        tile_values[0, 0], tile_rows[0], tile_cols[0], tile_count, n_col * nodes // TILE, n_row * nodes // TILE
    )
    terms = first_terms(ids, dense, sources, n_col)
    arrived = [terms[0]] + [swap(terms[k], "col", k) for k in range(1, n_col)]
    first_agg = tree_sum(arrived).astype(bf16)
    pieces = gather_row(first_agg)
    hidden, column, term = hidden_terms(
        ids, dense, hidden_weight, bias, class_lanes, code, pieces, n_col, lines
    )
    class_terms = [term] + [swap(term, "col", k) for k in range(1, n_col)]
    slope, turned = slopes(ids, hidden_weight, bias, pieces)
    logits, keep, send = gradients(
        ids, dense, column, slope, turned, class_turned, class_bias_lines, class_terms, classes
    )
    part = keep.astype(WIRE).astype(f32) + swap(send.astype(WIRE), "row", 1).astype(f32)
    part = sum_over(part, "row", 1, row_bits)
    part = sum_over(part, "col", 0, col_bits)
    mine = part.astype(WIRE)
    other = swap(mine, "row", 1)
    loss, weight_grad, bias_grad, class_grad, class_bias_grad = finish(
        ids, mine, other, features, lines, classes
    )
    return (
        hidden,
        logits,
        loss[0, 0],
        weight_grad,
        bias_grad[0],
        class_grad,
        class_bias_grad[0],
    )


def solution(mesh):
    in_specs = (
        P(("row", "col"), None),
        P("row", "col", None, None, None),
        P("row", "col", None),
        P("row", "col", None),
        P("row", "col"),
        P(("row", "col")),
        P(("row", "col")),
        P(),
        P(),
        P(),
        P(),
    )
    out_specs = (P(("row", "col"), None), P(None, ("row", "col")), P(), P(), P(), P(), P())
    return jax.shard_map(
        on_device, mesh=mesh, in_specs=in_specs, out_specs=out_specs, check_vma=False
    )
```

```python
import functools
import math

import jax
import jax.numpy as jnp
from jax import lax
from jax.experimental import pallas as pl
from jax.experimental.pallas import tpu as pltpu
from jax.sharding import PartitionSpec as P

TILE = 128
MASK_CODE = 128
MIB = 1024 * 1024
WIRE = jnp.bfloat16
f32 = jnp.float32
bf16 = jnp.bfloat16


VMEM = pl.BlockSpec(memory_space=pltpu.VMEM)
SMEM = pl.BlockSpec(memory_space=pltpu.SMEM)
HBM = pl.BlockSpec(memory_space=pltpu.HBM)


def params(limit):
    return pltpu.CompilerParams(vmem_limit_bytes=limit)


def cost(flops, moved, transcendentals=0):
    return pl.CostEstimate(flops=flops, bytes_accessed=moved, transcendentals=transcendentals)


def dot(a, b, dims=((1,), (0,))):
    return lax.dot_general(a, b, (dims, ((), ())), preferred_element_type=f32)


def halves(value):
    high = value.astype(bf16)
    return high, (value - high.astype(f32)).astype(bf16)


def densify_kernel(group, depth, banks, tile_rows, tile_cols, rows, cols, count, values, out, ring, *rest):
    totals, sem = rest[:banks], rest[banks]
    live = count[0, 0]
    groups = (live + group - 1) // group
    spare = tile_rows * tile_cols

    def copy(index, slot):
        return pltpu.make_async_copy(
            values.at[pl.ds(index * group, group)], ring.at[slot], sem.at[slot]
        )

    for slot in range(depth):
        @pl.when(slot < groups)
        def _():
            copy(slot, slot).start()

    for total in totals:
        @pl.loop(0, spare)
        def _(place):
            total[place] = jnp.zeros((TILE, TILE), f32)

    @pl.loop(0, groups)
    def _(index):
        slot = lax.rem(index, depth)
        copy(index, slot).wait()
        for k in range(group):
            item = index * group + k
            place = rows[0, item] * tile_cols + cols[0, item]
            place = jnp.where(item < live, place, spare)
            total = totals[k % banks]
            total[place] = total[place] + ring[slot, k].astype(f32)

        @pl.when(index + depth < groups)
        def _():
            copy(index + depth, slot).start()

    for tile_row in range(tile_rows):
        @pl.loop(0, tile_cols)
        def _(tile_col):
            place = tile_row * tile_cols + tile_col
            summed = functools.reduce(lambda a, b: a + b, [total[place] for total in totals])
            lanes = pl.ds(pl.multiple_of(tile_col * TILE, TILE), TILE)
            out[pl.ds(tile_row * TILE, TILE), lanes] = summed.astype(bf16)


def densify(values, rows, cols, count, tile_rows, tile_cols):
    slots = values.shape[0]
    group = math.gcd(slots, 16)
    places = tile_rows * tile_cols
    banks = 2 if places <= 128 else 1
    depth = min(slots // group, 8)
    return pl.pallas_call(
        functools.partial(densify_kernel, group, depth, banks, tile_rows, tile_cols),
        out_shape=jax.ShapeDtypeStruct((tile_rows * TILE, tile_cols * TILE), bf16),
        in_specs=[SMEM, SMEM, SMEM, HBM],
        out_specs=VMEM,
        scratch_shapes=[pltpu.VMEM((depth, group, TILE, TILE), bf16)]
        + [pltpu.VMEM((places + 1, TILE, TILE), f32) for _ in range(banks)]
        + [pltpu.SemaphoreType.DMA((depth,))],
        compiler_params=params(54 * MIB),
        cost_estimate=cost(slots * TILE * TILE, slots * TILE * TILE * 2),
        name="densify",
    )(rows, cols, count, values)


def first_kernel(n_row, n_col, ids, dense, *refs):
    pieces, outs, stacked = refs[:n_row], refs[n_row : n_row + n_col], refs[n_row + n_col]
    nodes = pieces[0].shape[0]
    row, col = ids[0], ids[1]
    for k in range(n_row):
        place = pl.multiple_of((row ^ k) * nodes, nodes)
        stacked[pl.ds(place, nodes), :] = pieces[k][...]
    for k in range(n_col):
        place = pl.multiple_of((col ^ k) * nodes, nodes)
        outs[k][...] = dot(dense[pl.ds(place, nodes), :], stacked[...]).astype(bf16)


def first_terms(ids, dense, pieces, n_col):
    nodes, width = pieces[0].shape
    n_row = len(pieces)
    return pl.pallas_call(
        functools.partial(first_kernel, n_row, n_col),
        out_shape=[jax.ShapeDtypeStruct((nodes, width), bf16)] * n_col,
        in_specs=[SMEM, VMEM] + [VMEM] * n_row,
        out_specs=[VMEM] * n_col,
        scratch_shapes=[pltpu.VMEM((n_row * nodes, width), bf16)],
        compiler_params=params(dense.size * 2 + 6 * MIB),
        cost_estimate=cost(2 * dense.size * width, dense.size * 2),
        name="first_terms",
    )(ids, dense, *pieces)


def hidden_kernel(n_row, n_col, ids, dense, weight, bias, class_weight, code, *refs):
    pieces = refs[:n_row]
    hidden_out, column_out, term_out, stacked = refs[n_row:]
    nodes = pieces[0].shape[0]
    row, col = ids[0], ids[1]
    for k in range(n_row):
        pre = dot(pieces[k][...], weight[...]) + bias[...]
        hidden = (pre * (1.0 / (1.0 + jnp.exp(-pre)))).astype(bf16)
        place = pl.multiple_of((row ^ k) * nodes, nodes)
        column_out[pl.ds(place, nodes), :] = hidden
        if k == 0:
            hidden_out[...] = hidden
        high, low = halves(dot(hidden, class_weight[...], ((1,), (1,))))
        stacked[pl.ds(place, nodes), :] = jnp.concatenate([high, low], axis=1)
    both = dot(dense[...], stacked[...])
    lanes = both.shape[1] // 2
    term = (both[:, :lanes] + both[:, lanes:]).T[: term_out.shape[0]]
    slice_of = lax.broadcasted_iota(jnp.int32, term.shape, 1) // nodes
    line = lax.broadcasted_iota(jnp.int32, term.shape, 0)
    codes = jnp.where(slice_of == col, jnp.concatenate([code[...]] * n_col, axis=1), 0.0)
    term_out[...] = jnp.where(line == term.shape[0] - 1, codes, term).astype(bf16)


def hidden_terms(ids, dense, weight, bias, class_weight, code, pieces, n_col, lines):
    nodes = pieces[0].shape[0]
    n_row = len(pieces)
    width = weight.shape[1]
    lanes = class_weight.shape[0]
    column = n_row * nodes
    return pl.pallas_call(
        functools.partial(hidden_kernel, n_row, n_col),
        out_shape=[
            jax.ShapeDtypeStruct((nodes, width), bf16),
            jax.ShapeDtypeStruct((column, width), bf16),
            jax.ShapeDtypeStruct((lines, n_col * nodes), bf16),
        ],
        in_specs=[SMEM] + [VMEM] * (5 + n_row),
        out_specs=[VMEM] * 3,
        scratch_shapes=[pltpu.VMEM((column, 2 * lanes), bf16)],
        compiler_params=params(dense.size * 2 + column * width * 8 + 6 * MIB),
        cost_estimate=cost(4 * dense.size * lanes, dense.size * 2, column * width * 2),
        name="hidden_terms",
    )(ids, dense, weight, bias, class_weight, code, *pieces)


def slope_kernel(n_row, ids, weight, bias, *refs):
    pieces = refs[:n_row]
    slope_out, turned_out = refs[n_row:]
    nodes = pieces[0].shape[0]
    row = ids[0]
    for k in range(n_row):
        pre = dot(pieces[k][...], weight[...]) + bias[...]
        sigma = 1.0 / (1.0 + jnp.exp(-pre))
        place = pl.multiple_of((row ^ k) * nodes, nodes)
        slope_out[pl.ds(place, nodes), :] = sigma * (1.0 + pre * (1.0 - sigma))
        turned_out[:, pl.ds(place, nodes)] = pieces[k][...].T


def slopes(ids, weight, bias, pieces):
    nodes, features = pieces[0].shape
    n_row = len(pieces)
    width = weight.shape[1]
    column = n_row * nodes
    return pl.pallas_call(
        functools.partial(slope_kernel, n_row),
        out_shape=[
            jax.ShapeDtypeStruct((column, width), f32),
            jax.ShapeDtypeStruct((features, column), bf16),
        ],
        in_specs=[SMEM] + [VMEM] * (2 + n_row),
        out_specs=[VMEM] * 2,
        compiler_params=params(column * width * 8 + 4 * MIB),
        cost_estimate=cost(2 * column * features * width, column * width * 4, column * width * 2),
        name="slopes",
    )(ids, weight, bias, *pieces)


def tree_sum(parts):
    parts = [part.astype(f32) for part in parts]
    while len(parts) > 1:
        parts = [parts[k] + parts[k + 1] for k in range(0, len(parts), 2)]
    return parts[0]


def gradient_kernel(n_col, classes, ids, dense, column, slope, turned, class_weight_turned, class_bias, *refs):
    terms = refs[:n_col]
    logits_out, keep_out, send_out, scratch, packed = refs[n_col:]
    lines, nodes_row = terms[0].shape
    nodes = nodes_row // n_col
    features = turned.shape[0]
    width = column.shape[1]
    row, col = ids[0], ids[1]
    total = tree_sum([term[...] for term in terms])
    code = total[lines - 1 :, :]
    live = (code >= MASK_CODE).astype(f32)
    label = (code - MASK_CODE * live).astype(jnp.int32)
    line = lax.broadcasted_iota(jnp.int32, total.shape, 0)
    bias = jnp.broadcast_to(class_bias[...], (8, class_bias.shape[1])).T[:lines, :1]
    logits = jnp.where(line < classes, total + bias, -jnp.inf)
    scratch[...] = logits
    own = pl.ds(pl.multiple_of(col * nodes, nodes), nodes)
    logits_out[...] = scratch[:classes, own]
    top = jnp.max(logits, axis=0, keepdims=True)
    log_total = top + jnp.log(jnp.sum(jnp.exp(logits - top), axis=0, keepdims=True))
    chosen = line == label
    picked = jnp.sum(jnp.where(chosen, logits, 0.0), axis=0, keepdims=True)
    grad = (jnp.exp(logits - log_total) - chosen.astype(f32)) * live
    high, low = halves(grad)
    stacked = jnp.concatenate([high, low], axis=0)
    both = dot(stacked, dense[...])
    back = both[:lines] + both[lines:]
    back_high, back_low = halves(back)
    back_both = jnp.concatenate([back_high, back_low], axis=0)
    class_both = dot(back_both, column[...])
    packed[pl.ds(features, lines), :] = class_both[:lines] + class_both[lines:]
    twice = jnp.concatenate([class_weight_turned[:lines, :]] * 2, axis=0)
    hidden_grad = dot(back_both, twice, ((0,), (0,)))
    pre_grad = hidden_grad * slope[...]
    pre_high, pre_low = halves(pre_grad)
    packed[pl.ds(0, features), :] = dot(turned[...], pre_high) + dot(turned[...], pre_low)
    packed[pl.ds(features + lines - 1, 1), :] = jnp.sum(pre_grad, axis=0, keepdims=True)
    here = (lax.broadcasted_iota(jnp.int32, (8, nodes_row), 1) // nodes == col).astype(f32)
    ours = here.astype(bf16)
    class_sum = dot(ours, high, ((1,), (1,))) + dot(ours, low, ((1,), (1,)))
    class_sum = jnp.concatenate([class_sum, jnp.zeros((8, width - lines), f32)], axis=1)
    loss = jnp.sum((log_total - picked) * live * here[:1])
    members = jnp.sum(live * here[:1])
    lane = lax.broadcasted_iota(jnp.int32, (8, width), 1)
    entry = lax.broadcasted_iota(jnp.int32, (8, width), 0)
    loss = jnp.full((8, width), loss, f32)
    loss_high = loss.astype(bf16).astype(f32)
    loss_middle = (loss - loss_high).astype(bf16).astype(f32)
    loss_low = loss - loss_high - loss_middle
    values = jnp.where(entry == 0, loss_high, jnp.where(entry == 1, loss_middle, loss_low))
    values = jnp.where(entry == 3, members, jnp.where(entry < 3, values, 0.0))
    tail = jnp.where(lane == row * n_col + col, values, 0.0)
    packed[pl.ds(features + lines, 8), :] = class_sum
    packed[pl.ds(features + lines + 8, 8), :] = tail
    part = packed.shape[0] // 2
    core = row & 1
    keep_out[...] = packed[pl.ds(pl.multiple_of(core * part, 8), part), :].astype(keep_out.dtype)
    send_out[...] = packed[pl.ds(pl.multiple_of((1 - core) * part, 8), part), :].astype(send_out.dtype)


def gradients(ids, dense, column, slope, turned, class_weight_turned, class_bias, terms, classes):
    n_col = len(terms)
    lines, nodes_row = terms[0].shape
    width = column.shape[1]
    packed = turned.shape[0] + lines + 16
    return pl.pallas_call(
        functools.partial(gradient_kernel, n_col, classes),
        out_shape=[
            jax.ShapeDtypeStruct((classes, nodes_row // n_col), f32),
            jax.ShapeDtypeStruct((packed // 2, width), WIRE),
            jax.ShapeDtypeStruct((packed // 2, width), WIRE),
        ],
        in_specs=[SMEM] + [VMEM] * (6 + n_col),
        out_specs=[VMEM] * 3,
        scratch_shapes=[
            pltpu.VMEM((lines, nodes_row), f32),
            pltpu.VMEM((packed, width), f32),
        ],
        compiler_params=params(dense.size * 2 + column.size * 16 + 6 * MIB),
        cost_estimate=cost(4 * dense.size * lines, dense.size * 2),
        name="gradients",
    )(ids, dense, column, slope, turned, class_weight_turned, class_bias, *terms)


def finish_kernel(features, lines, classes, ids, mine, other, loss_out, weight_out, bias_out, class_out, class_bias_out, packed):
    part = mine.shape[0]
    core = ids[0] & 1
    packed[pl.ds(pl.multiple_of(core * part, 8), part), :] = mine[...].astype(f32)
    packed[pl.ds(pl.multiple_of((1 - core) * part, 8), part), :] = other[...].astype(f32)
    tail = packed[pl.ds(features + lines + 8, 8), :]
    sums = jnp.sum(tail, axis=1, keepdims=True)
    members = sums[3:4]
    loss_out[...] = (sums[0:1] + sums[1:2] + sums[2:3]) / members
    weight_out[...] = packed[pl.ds(0, features), :] / members
    bias_out[...] = packed[pl.ds(features + lines - 1, 1), :] / members
    class_out[...] = packed[pl.ds(features, classes), :] / members
    class_bias_out[...] = packed[pl.ds(features + lines, 1), :][:, :classes] / members


def finish(ids, mine, other, features, lines, classes):
    part, width = mine.shape
    return pl.pallas_call(
        functools.partial(finish_kernel, features, lines, classes),
        out_shape=[
            jax.ShapeDtypeStruct((1, 1), f32),
            jax.ShapeDtypeStruct((features, width), f32),
            jax.ShapeDtypeStruct((1, width), f32),
            jax.ShapeDtypeStruct((classes, width), f32),
            jax.ShapeDtypeStruct((1, classes), f32),
        ],
        in_specs=[SMEM, VMEM, VMEM],
        out_specs=[VMEM] * 5,
        scratch_shapes=[pltpu.VMEM((2 * part, width), f32)],
        compiler_params=params(4 * MIB),
        name="finish",
    )(ids, mine, other)


def swap(value, axis, mask):
    size = lax.axis_size(axis)
    return lax.ppermute(value, axis, [(k, k ^ mask) for k in range(size)])


def gather_row(value):
    size = lax.axis_size("row")
    even = [value] + [swap(value, "row", k) for k in range(2, size, 2)]
    odd = [swap(piece, "row", 1) for piece in even]
    return [piece for pair in zip(even, odd) for piece in pair]


def sum_over(value, axis, low, high):
    while low < high:
        step = min(2, high - low)
        parts = [value.astype(WIRE)]
        parts += [swap(parts[0], axis, k << low) for k in range(1, 1 << step)]
        value = tree_sum(parts)
        low += step
    return value


def on_device(
    node_features,
    tile_values,
    tile_rows,
    tile_cols,
    tile_count,
    labels,
    train_mask,
    hidden_weight,
    hidden_bias,
    class_weight,
    class_bias,
):
    nodes, features = node_features.shape
    classes = class_weight.shape[1]
    n_row, n_col = lax.axis_size("row"), lax.axis_size("col")
    row_bits, col_bits = n_row.bit_length() - 1, n_col.bit_length() - 1
    lines = (classes // 16 + 1) * 16
    ids = jnp.stack([lax.axis_index("row"), lax.axis_index("col")]).astype(jnp.int32)
    code = (labels + MASK_CODE * train_mask).astype(f32)[None, :]
    bias = hidden_bias[None, :]
    class_turned = jnp.pad(class_weight.T, ((0, TILE - classes), (0, 0)))
    class_bias_lanes = jnp.pad(class_bias, (0, TILE - classes))[None, :]

    sources = gather_row(node_features)
    dense = densify(
        tile_values[0, 0], tile_rows[0], tile_cols[0], tile_count, n_col * nodes // TILE, n_row * nodes // TILE
    )
    terms = first_terms(ids, dense, sources, n_col)
    arrived = [terms[0]] + [swap(terms[k], "col", k) for k in range(1, n_col)]
    first_agg = tree_sum(arrived).astype(bf16)
    pieces = gather_row(first_agg)
    hidden, column, term = hidden_terms(
        ids, dense, hidden_weight, bias, class_turned, code, pieces, n_col, lines
    )
    class_terms = [term] + [swap(term, "col", k) for k in range(1, n_col)]
    slope, turned = slopes(ids, hidden_weight, bias, pieces)
    logits, keep, send = gradients(
        ids, dense, column, slope, turned, class_turned, class_bias_lanes, class_terms, classes
    )
    part = keep.astype(f32) + swap(send, "row", 1).astype(f32)
    part = sum_over(part, "row", 1, row_bits)
    part = sum_over(part, "col", 0, col_bits)
    mine = part.astype(WIRE)
    other = swap(mine, "row", 1)
    loss, weight_grad, bias_grad, class_grad, class_bias_grad = finish(
        ids, mine, other, features, lines, classes
    )
    return (
        hidden,
        logits,
        loss[0, 0],
        weight_grad,
        bias_grad[0],
        class_grad.T,
        class_bias_grad[0],
    )


def solution(mesh):
    in_specs = (
        P(("row", "col"), None),
        P("row", "col", None, None, None),
        P("row", "col", None),
        P("row", "col", None),
        P("row", "col"),
        P(("row", "col")),
        P(("row", "col")),
        P(),
        P(),
        P(),
        P(),
    )
    out_specs = (P(("row", "col"), None), P(None, ("row", "col")), P(), P(), P(), P(), P())
    return jax.shard_map(
        on_device, mesh=mesh, in_specs=in_specs, out_specs=out_specs, check_vma=False
    )
```

```python
import functools
import math

import jax
import jax.numpy as jnp
from jax import lax
from jax.experimental import pallas as pl
from jax.experimental.pallas import tpu as pltpu
from jax.sharding import PartitionSpec as P


TILE = 128
MASK_CODE = 128
MIB = 1024 * 1024
WIRE = jnp.bfloat16
f32 = jnp.float32
bf16 = jnp.bfloat16


VMEM = pl.BlockSpec(memory_space=pltpu.VMEM)
SMEM = pl.BlockSpec(memory_space=pltpu.SMEM)
HBM = pl.BlockSpec(memory_space=pltpu.HBM)


def params(limit):
    return pltpu.CompilerParams(vmem_limit_bytes=limit)


def cost(flops, moved, transcendentals=0):
    return pl.CostEstimate(flops=flops, bytes_accessed=moved, transcendentals=transcendentals)


def dot(a, b, dims=((1,), (0,))):
    return lax.dot_general(a, b, (dims, ((), ())), preferred_element_type=f32)


def halves(value):
    high = value.astype(bf16)
    return high, (value - high.astype(f32)).astype(bf16)


def collect_kernel(group, depth, places, values, total, ring, sem):
    slots = values.shape[0]
    groups = slots // group
    spare = total.shape[0] - 1
    count = places[0, slots]
    live = (count + group - 1) // group

    def copy(index, slot):
        return pltpu.make_async_copy(
            values.at[pl.ds(index * group, group)], ring.at[slot], sem.at[slot]
        )

    for slot in range(depth):
        @pl.when(slot < live)
        def _():
            copy(slot, slot).start()

    @pl.loop(0, spare // 4)
    def _(place):
        for k in range(4):
            total[place * 4 + k] = jnp.zeros((TILE, TILE), f32)

    @pl.loop(0, live)
    def _(index):
        slot = lax.rem(index, depth)
        copy(index, slot).wait()
        for k in range(group):
            place = places[0, index * group + k]
            total[place] = total[place] + ring[slot, k].astype(f32)

        if depth < groups:
            @pl.when(index + depth < live)
            def _():
                copy(index + depth, slot).start()


def collect(values, places, n_places):
    slots = values.shape[0]
    group = math.gcd(slots, 16)
    small = n_places <= 128
    depth = slots // group if small else min(slots // group, 8)
    return pl.pallas_call(
        functools.partial(collect_kernel, group, depth),
        out_shape=jax.ShapeDtypeStruct((n_places + 1, TILE, TILE), f32),
        in_specs=[SMEM, HBM],
        out_specs=VMEM,
        scratch_shapes=[
            pltpu.VMEM((depth, group, TILE, TILE), bf16),
            pltpu.SemaphoreType.DMA((depth,)),
        ],
        compiler_params=params((44 if small else 56) * MIB),
        cost_estimate=cost(slots * TILE * TILE, slots * TILE * TILE * 2),
        name="collect",
    )(places, values)


def position(row, k, n_row):
    other = row ^ k
    return (other & 1) * (n_row // 2) + (other >> 1)


def place_of(row, k, n_row, nodes):
    return pl.ds(pl.multiple_of(position(row, k, n_row) * nodes, nodes), nodes)


def stack(row, start, pieces, stacked):
    nodes = pieces[0].shape[0]
    for k, piece in enumerate(pieces):
        place = pl.multiple_of(((row ^ (start + 2 * k)) >> 1) * nodes, nodes)
        stacked[pl.ds(place, nodes), :] = piece[...]


def parity_columns(parity, columns):
    return pl.ds(pl.multiple_of(parity * (columns // 2), columns // 2), columns // 2)


def first_near_kernel(n_row, ids, total, *refs):
    pieces = refs[: n_row // 2]
    dense, part, stacked = refs[n_row // 2 :]
    row = ids[0]
    stack(row, 0, pieces, stacked)
    tile_rows = dense.shape[0] // TILE
    tile_cols = dense.shape[1] // TILE
    each = tile_cols // n_row
    for tile_row in range(tile_rows):
        @pl.loop(0, tile_cols)
        def _(tile_col):
            source = tile_col // each
            target = position(source, 0, n_row) * each + tile_col % each
            lanes = pl.ds(pl.multiple_of(target * TILE, TILE), TILE)
            dense[tile_row * TILE : (tile_row + 1) * TILE, lanes] = total[tile_row * tile_cols + tile_col].astype(bf16)
    part[...] = dot(dense[:, parity_columns(row & 1, dense.shape[1])], stacked[...])


def first_near(ids, total, pieces, n_col):
    nodes, width = pieces[0].shape
    n_row = 2 * len(pieces)
    size = (n_col * nodes, n_row * nodes)
    return pl.pallas_call(
        functools.partial(first_near_kernel, n_row),
        out_shape=[jax.ShapeDtypeStruct(size, bf16), jax.ShapeDtypeStruct((size[0], width), f32)],
        in_specs=[SMEM, VMEM] + [VMEM] * len(pieces),
        out_specs=[VMEM] * 2,
        scratch_shapes=[pltpu.VMEM((len(pieces) * nodes, width), bf16)],
        compiler_params=params(size[0] * size[1] * 6 + 6 * MIB),
        cost_estimate=cost(size[0] * size[1] * width, size[0] * size[1] * 6),
        name="first_near",
    )(ids, total, *pieces)


def first_far_kernel(n_row, n_col, ids, dense, part, *refs):
    pieces = refs[: n_row // 2]
    outs, stacked = refs[n_row // 2 : -1], refs[-1]
    nodes = pieces[0].shape[0]
    row, col = ids[0], ids[1]
    stack(row, 1, pieces, stacked)
    columns = parity_columns(1 - (row & 1), dense.shape[1])
    for k in range(n_col):
        lines = pl.ds(pl.multiple_of((col ^ k) * nodes, nodes), nodes)
        outs[k][...] = (part[lines, :] + dot(dense[lines, columns], stacked[...])).astype(bf16)


def first_far(ids, dense, part, pieces, n_col):
    nodes, width = pieces[0].shape
    n_row = 2 * len(pieces)
    return pl.pallas_call(
        functools.partial(first_far_kernel, n_row, n_col),
        out_shape=[jax.ShapeDtypeStruct((nodes, width), bf16)] * n_col,
        in_specs=[SMEM, VMEM, VMEM] + [VMEM] * len(pieces),
        out_specs=[VMEM] * n_col,
        scratch_shapes=[pltpu.VMEM((len(pieces) * nodes, width), bf16)],
        compiler_params=params(dense.size * 2 + 6 * MIB),
        cost_estimate=cost(dense.size * width, dense.size),
        name="first_far",
    )(ids, dense, part, *pieces)


def hidden_kernel(n_row, n_col, ids, dense, weight, bias, class_weight, code, *refs):
    pieces = refs[:n_row]
    hidden_out, column_out, term_out, stacked = refs[n_row:]
    nodes = pieces[0].shape[0]
    row, col = ids[0], ids[1]
    for k in range(n_row):
        pre = dot(pieces[k][...], weight[...]) + bias[...]
        hidden = (pre * (1.0 / (1.0 + jnp.exp(-pre)))).astype(bf16)
        place = place_of(row, k, n_row, nodes)
        column_out[place, :] = hidden
        if k == 0:
            hidden_out[...] = hidden
        high, low = halves(dot(hidden, class_weight[...], ((1,), (1,))))
        stacked[place, :] = jnp.concatenate([high, low], axis=1)
    both = dot(dense[...], stacked[...])
    lanes = both.shape[1] // 2
    term = (both[:, :lanes] + both[:, lanes:]).T[: term_out.shape[0]]
    slice_of = lax.broadcasted_iota(jnp.int32, term.shape, 1) // nodes
    line = lax.broadcasted_iota(jnp.int32, term.shape, 0)
    codes = jnp.where(slice_of == col, jnp.concatenate([code[...]] * n_col, axis=1), 0.0)
    term_out[...] = jnp.where(line == term.shape[0] - 1, codes, term).astype(bf16)


def hidden_terms(ids, dense, weight, bias, class_weight, code, pieces, n_col, lines):
    nodes = pieces[0].shape[0]
    n_row = len(pieces)
    width = weight.shape[1]
    lanes = class_weight.shape[0]
    column = n_row * nodes
    return pl.pallas_call(
        functools.partial(hidden_kernel, n_row, n_col),
        out_shape=[
            jax.ShapeDtypeStruct((nodes, width), bf16),
            jax.ShapeDtypeStruct((column, width), bf16),
            jax.ShapeDtypeStruct((lines, n_col * nodes), bf16),
        ],
        in_specs=[SMEM] + [VMEM] * (5 + n_row),
        out_specs=[VMEM] * 3,
        scratch_shapes=[pltpu.VMEM((column, 2 * lanes), bf16)],
        compiler_params=params(dense.size * 2 + column * width * 8 + 6 * MIB),
        cost_estimate=cost(4 * dense.size * lanes, dense.size * 2, column * width * 2),
        name="hidden_terms",
    )(ids, dense, weight, bias, class_weight, code, *pieces)


def slope_kernel(n_row, ids, weight, bias, *refs):
    pieces = refs[:n_row]
    slope_out, turned_out = refs[n_row:]
    nodes = pieces[0].shape[0]
    row = ids[0]
    for k in range(n_row):
        pre = dot(pieces[k][...], weight[...]) + bias[...]
        sigma = 1.0 / (1.0 + jnp.exp(-pre))
        place = place_of(row, k, n_row, nodes)
        slope_out[place, :] = sigma * (1.0 + pre * (1.0 - sigma))
        turned_out[:, place] = pieces[k][...].T


def slopes(ids, weight, bias, pieces):
    nodes, features = pieces[0].shape
    n_row = len(pieces)
    width = weight.shape[1]
    column = n_row * nodes
    return pl.pallas_call(
        functools.partial(slope_kernel, n_row),
        out_shape=[
            jax.ShapeDtypeStruct((column, width), f32),
            jax.ShapeDtypeStruct((features, column), bf16),
        ],
        in_specs=[SMEM] + [VMEM] * (2 + n_row),
        out_specs=[VMEM] * 2,
        compiler_params=params(column * width * 8 + 4 * MIB),
        cost_estimate=cost(2 * column * features * width, column * width * 4, column * width * 2),
        name="slopes",
    )(ids, weight, bias, *pieces)


def tree_sum(parts):
    parts = [part.astype(f32) for part in parts]
    while len(parts) > 1:
        parts = [parts[k] + parts[k + 1] for k in range(0, len(parts), 2)]
    return parts[0]


def gradient_kernel(n_col, classes, ids, dense, column, slope, turned, class_weight_turned, class_bias, *refs):
    terms = refs[:n_col]
    logits_out, keep_out, send_out, scratch, packed = refs[n_col:]
    lines, nodes_row = terms[0].shape
    nodes = nodes_row // n_col
    features = turned.shape[0]
    width = column.shape[1]
    row, col = ids[0], ids[1]
    total = tree_sum([term[...] for term in terms])
    code = total[lines - 1 :, :]
    live = (code >= MASK_CODE).astype(f32)
    label = (code - MASK_CODE * live).astype(jnp.int32)
    line = lax.broadcasted_iota(jnp.int32, total.shape, 0)
    bias = jnp.broadcast_to(class_bias[...], (8, class_bias.shape[1])).T[:lines, :1]
    logits = jnp.where(line < classes, total + bias, -jnp.inf)
    scratch[...] = logits
    own = pl.ds(pl.multiple_of(col * nodes, nodes), nodes)
    logits_out[...] = scratch[:classes, own]
    top = jnp.max(logits, axis=0, keepdims=True)
    log_total = top + jnp.log(jnp.sum(jnp.exp(logits - top), axis=0, keepdims=True))
    chosen = line == label
    picked = jnp.sum(jnp.where(chosen, logits, 0.0), axis=0, keepdims=True)
    grad = (jnp.exp(logits - log_total) - chosen.astype(f32)) * live
    high, low = halves(grad)
    stacked = jnp.concatenate([high, low], axis=0)
    both = dot(stacked, dense[...])
    back = both[:lines] + both[lines:]
    back_high, back_low = halves(back)
    back_both = jnp.concatenate([back_high, back_low], axis=0)
    class_both = dot(back_both, column[...])
    packed[pl.ds(features, lines), :] = class_both[:lines] + class_both[lines:]
    twice = jnp.concatenate([class_weight_turned[:lines, :]] * 2, axis=0)
    hidden_grad = dot(back_both, twice, ((0,), (0,)))
    pre_grad = hidden_grad * slope[...]
    pre_high, pre_low = halves(pre_grad)
    packed[pl.ds(0, features), :] = dot(turned[...], pre_high) + dot(turned[...], pre_low)
    packed[pl.ds(features + lines - 1, 1), :] = jnp.sum(pre_grad, axis=0, keepdims=True)
    here = (lax.broadcasted_iota(jnp.int32, (8, nodes_row), 1) // nodes == col).astype(f32)
    ours = here.astype(bf16)
    class_sum = dot(ours, high, ((1,), (1,))) + dot(ours, low, ((1,), (1,)))
    class_sum = jnp.concatenate([class_sum, jnp.zeros((8, width - lines), f32)], axis=1)
    loss = jnp.sum((log_total - picked) * live * here[:1])
    members = jnp.sum(live * here[:1])
    lane = lax.broadcasted_iota(jnp.int32, (8, width), 1)
    entry = lax.broadcasted_iota(jnp.int32, (8, width), 0)
    loss = jnp.full((8, width), loss, f32)
    loss_high = loss.astype(bf16).astype(f32)
    loss_middle = (loss - loss_high).astype(bf16).astype(f32)
    loss_low = loss - loss_high - loss_middle
    values = jnp.where(entry == 0, loss_high, jnp.where(entry == 1, loss_middle, loss_low))
    values = jnp.where(entry == 3, members, jnp.where(entry < 3, values, 0.0))
    tail = jnp.where(lane == row * n_col + col, values, 0.0)
    packed[pl.ds(features + lines, 8), :] = class_sum
    packed[pl.ds(features + lines + 8, 8), :] = tail
    part = packed.shape[0] // 2
    core = row & 1
    keep_out[...] = packed[pl.ds(pl.multiple_of(core * part, 8), part), :].astype(keep_out.dtype)
    send_out[...] = packed[pl.ds(pl.multiple_of((1 - core) * part, 8), part), :].astype(send_out.dtype)


def gradients(ids, dense, column, slope, turned, class_weight_turned, class_bias, terms, classes):
    n_col = len(terms)
    lines, nodes_row = terms[0].shape
    width = column.shape[1]
    packed = turned.shape[0] + lines + 16
    return pl.pallas_call(
        functools.partial(gradient_kernel, n_col, classes),
        out_shape=[
            jax.ShapeDtypeStruct((classes, nodes_row // n_col), f32),
            jax.ShapeDtypeStruct((packed // 2, width), WIRE),
            jax.ShapeDtypeStruct((packed // 2, width), WIRE),
        ],
        in_specs=[SMEM] + [VMEM] * (6 + n_col),
        out_specs=[VMEM] * 3,
        scratch_shapes=[
            pltpu.VMEM((lines, nodes_row), f32),
            pltpu.VMEM((packed, width), f32),
        ],
        compiler_params=params(dense.size * 2 + column.size * 16 + 6 * MIB),
        cost_estimate=cost(4 * dense.size * lines, dense.size * 2),
        name="gradients",
    )(ids, dense, column, slope, turned, class_weight_turned, class_bias, *terms)


def finish_kernel(features, lines, classes, ids, mine, other, loss_out, weight_out, bias_out, class_out, class_bias_out, packed):
    part = mine.shape[0]
    core = ids[0] & 1
    packed[pl.ds(pl.multiple_of(core * part, 8), part), :] = mine[...].astype(f32)
    packed[pl.ds(pl.multiple_of((1 - core) * part, 8), part), :] = other[...].astype(f32)
    tail = packed[pl.ds(features + lines + 8, 8), :]
    sums = jnp.sum(tail, axis=1, keepdims=True)
    members = sums[3:4]
    loss_out[...] = (sums[0:1] + sums[1:2] + sums[2:3]) / members
    weight_out[...] = packed[pl.ds(0, features), :] / members
    bias_out[...] = packed[pl.ds(features + lines - 1, 1), :] / members
    class_out[...] = packed[pl.ds(features, classes), :] / members
    class_bias_out[...] = packed[pl.ds(features + lines, 1), :][:, :classes] / members


def finish(ids, mine, other, features, lines, classes):
    part, width = mine.shape
    return pl.pallas_call(
        functools.partial(finish_kernel, features, lines, classes),
        out_shape=[
            jax.ShapeDtypeStruct((1, 1), f32),
            jax.ShapeDtypeStruct((features, width), f32),
            jax.ShapeDtypeStruct((1, width), f32),
            jax.ShapeDtypeStruct((classes, width), f32),
            jax.ShapeDtypeStruct((1, classes), f32),
        ],
        in_specs=[SMEM, VMEM, VMEM],
        out_specs=[VMEM] * 5,
        scratch_shapes=[pltpu.VMEM((2 * part, width), f32)],
        compiler_params=params(4 * MIB),
        name="finish",
    )(ids, mine, other)


def swap(value, axis, mask):
    size = lax.axis_size(axis)
    return lax.ppermute(value, axis, [(k, k ^ mask) for k in range(size)])


def gather_row(value):
    size = lax.axis_size("row")
    even = [value] + [swap(value, "row", k) for k in range(2, size, 2)]
    odd = [swap(even[0], "row", 1)]
    odd += [swap(piece, "row", 1) for piece in even[1:]]
    return even, odd


def sum_over(value, axis, low, high):
    while low < high:
        step = min(2, high - low)
        parts = [value.astype(WIRE)]
        parts += [swap(parts[0], axis, k << low) for k in range(1, 1 << step)]
        value = tree_sum(parts)
        low += step
    return value


def step(
    node_features,
    tile_values,
    tile_rows,
    tile_cols,
    tile_count,
    labels,
    train_mask,
    hidden_weight,
    hidden_bias,
    class_weight,
    class_bias,
):
    nodes, features = node_features.shape
    classes = class_weight.shape[1]
    n_row, n_col = lax.axis_size("row"), lax.axis_size("col")
    row_bits, col_bits = n_row.bit_length() - 1, n_col.bit_length() - 1
    lines = (classes // 16 + 1) * 16
    ids = jnp.stack([lax.axis_index("row"), lax.axis_index("col")]).astype(jnp.int32)
    code = (labels + MASK_CODE * train_mask).astype(f32)[None, :]
    bias = hidden_bias[None, :]
    class_turned = jnp.pad(class_weight.T, ((0, TILE - classes), (0, 0)))
    class_bias_lanes = jnp.pad(class_bias, (0, TILE - classes))[None, :]

    tile_cols_here = n_row * nodes // TILE
    n_places = n_col * nodes // TILE * tile_cols_here
    slots = tile_values.shape[2]
    places = jnp.where(
        jnp.arange(slots)[None, :] < tile_count,
        tile_rows[0] * tile_cols_here + tile_cols[0],
        n_places,
    )
    places = jnp.concatenate([places, jnp.broadcast_to(tile_count, (1, TILE))], axis=1)

    near, far = gather_row(node_features)
    total = collect(tile_values[0, 0], places, n_places)
    dense, part = first_near(ids, total, near, n_col)
    terms = first_far(ids, dense, part, far, n_col)
    arrived = [terms[0]] + [swap(terms[k], "col", k) for k in range(1, n_col)]
    first_agg = tree_sum(arrived).astype(bf16)
    near, far = gather_row(first_agg)
    pieces = [piece for pair in zip(near, far) for piece in pair]
    hidden, column, term = hidden_terms(
        ids, dense, hidden_weight, bias, class_turned, code, pieces, n_col, lines
    )
    class_terms = [term] + [swap(term, "col", k) for k in range(1, n_col)]
    slope, turned = slopes(ids, hidden_weight, bias, pieces)
    logits, keep, send = gradients(
        ids, dense, column, slope, turned, class_turned, class_bias_lanes, class_terms, classes
    )
    part = keep.astype(f32) + swap(send, "row", 1).astype(f32)
    part = sum_over(part, "row", 1, row_bits)
    part = sum_over(part, "col", 0, col_bits)
    mine = part.astype(WIRE)
    other = swap(mine, "row", 1)
    loss, weight_grad, bias_grad, class_grad, class_bias_grad = finish(
        ids, mine, other, features, lines, classes
    )
    return (
        hidden,
        logits,
        loss[0, 0],
        weight_grad,
        bias_grad[0],
        class_grad.T,
        class_bias_grad[0],
    )


def solution(mesh):
    in_specs = (
        P(("row", "col"), None),
        P("row", "col", None, None, None),
        P("row", "col", None),
        P("row", "col", None),
        P("row", "col"),
        P(("row", "col")),
        P(("row", "col")),
        P(),
        P(),
        P(),
        P(),
    )
    out_specs = (P(("row", "col"), None), P(None, ("row", "col")), P(), P(), P(), P(), P())
    return jax.shard_map(step, mesh=mesh, in_specs=in_specs, out_specs=out_specs, check_vma=False)
```

```python
import functools
import math

import jax
import jax.numpy as jnp
from jax import lax
from jax.experimental import pallas as pl
from jax.experimental.pallas import tpu as pltpu
from jax.sharding import PartitionSpec as P


TILE = 128
MASK_CODE = 128
MIB = 1024 * 1024
WIRE = jnp.bfloat16
f32 = jnp.float32
bf16 = jnp.bfloat16


VMEM = pl.BlockSpec(memory_space=pltpu.VMEM)
SMEM = pl.BlockSpec(memory_space=pltpu.SMEM)
HBM = pl.BlockSpec(memory_space=pltpu.HBM)


def params(limit):
    return pltpu.CompilerParams(vmem_limit_bytes=limit)


def cost(flops, moved, transcendentals=0):
    return pl.CostEstimate(flops=flops, bytes_accessed=moved, transcendentals=transcendentals)


def dot(a, b, dims=((1,), (0,))):
    return lax.dot_general(a, b, (dims, ((), ())), preferred_element_type=f32)


def halves(value):
    high = value.astype(bf16)
    return high, (value - high.astype(f32)).astype(bf16)


def collect_kernel(group, depth, tile_cols, ids, count, rows_hbm, cols_hbm, values, total, ring, rows, cols, sem, table_sem):
    slots = values.shape[0]
    groups = slots // group
    spare = total.shape[0] - 1
    tables = [
        pltpu.make_async_copy(source, target, table_sem.at[k])
        for k, (source, target) in enumerate(((rows_hbm, rows), (cols_hbm, cols)))
    ]
    for table in tables:
        table.start()

    def copy(index, slot):
        return pltpu.make_async_copy(
            values.at[pl.ds(index * group, group)], ring.at[slot], sem.at[slot]
        )

    live = count[0, 0]
    groups_live = (live + group - 1) // group
    for slot in range(depth):
        @pl.when(slot < groups_live)
        def _():
            copy(slot, slot).start()

    @pl.loop(0, spare // 4)
    def _(place):
        for k in range(4):
            total[place * 4 + k] = jnp.zeros((TILE, TILE), f32)

    for table in tables:
        table.wait()

    @pl.loop(0, groups_live)
    def _(index):
        slot = lax.rem(index, depth)
        copy(index, slot).wait()
        for k in range(group):
            item = index * group + k
            place = rows[0, item] * tile_cols + cols[0, item]
            place = jnp.where(item < live, place, spare)
            total[place] = total[place] + ring[slot, k].astype(f32)

        if depth < groups:
            @pl.when(index + depth < groups_live)
            def _():
                copy(index + depth, slot).start()


def collect(ids, values, rows, cols, count, tile_rows, tile_cols):
    slots = values.shape[0]
    n_places = tile_rows * tile_cols
    group = math.gcd(slots, 16)
    small = n_places <= 128
    depth = slots // group if small else min(slots // group, 8)
    rows, cols = (pltpu.with_memory_space_constraint(x, pltpu.HBM) for x in (rows, cols))
    return pl.pallas_call(
        functools.partial(collect_kernel, group, depth, tile_cols),
        out_shape=jax.ShapeDtypeStruct((n_places + 1, TILE, TILE), f32),
        in_specs=[SMEM, SMEM, HBM, HBM, HBM],
        out_specs=VMEM,
        scratch_shapes=[
            pltpu.VMEM((depth, group, TILE, TILE), bf16),
            pltpu.SMEM((1, slots), jnp.int32),
            pltpu.SMEM((1, slots), jnp.int32),
            pltpu.SemaphoreType.DMA((depth,)),
            pltpu.SemaphoreType.DMA((2,)),
        ],
        compiler_params=params((44 if small else 56) * MIB),
        cost_estimate=cost(slots * TILE * TILE, slots * TILE * TILE * 2),
        name="collect",
    )(ids, count, rows, cols, values)


def position(row, k, n_row):
    other = row ^ k
    return (other & 1) * (n_row // 2) + (other >> 1)


def place_of(row, k, n_row, nodes):
    return pl.ds(pl.multiple_of(position(row, k, n_row) * nodes, nodes), nodes)


def stack(row, start, pieces, stacked):
    nodes = pieces[0].shape[0]
    for k, piece in enumerate(pieces):
        place = pl.multiple_of(((row ^ (start + 2 * k)) >> 1) * nodes, nodes)
        stacked[pl.ds(place, nodes), :] = piece[...]


def parity_columns(parity, columns):
    return pl.ds(pl.multiple_of(parity * (columns // 2), columns // 2), columns // 2)


def round_kernel(n_row, total, dense):
    tile_rows = dense.shape[0] // TILE
    tile_cols = dense.shape[1] // TILE
    each = tile_cols // n_row

    @pl.loop(0, tile_rows)
    def _(tile_row):
        lines = pl.ds(pl.multiple_of(tile_row * TILE, TILE), TILE)
        for tile_col in range(tile_cols):
            target = position(tile_col // each, 0, n_row) * each + tile_col % each
            lanes = pl.ds(target * TILE, TILE)
            dense[lines, lanes] = total[tile_row * tile_cols + tile_col].astype(bf16)


def round_block(total, lines, columns, n_row):
    return pl.pallas_call(
        functools.partial(round_kernel, n_row),
        out_shape=jax.ShapeDtypeStruct((lines, columns), bf16),
        in_specs=[VMEM],
        out_specs=VMEM,
        compiler_params=params(lines * columns * 6 + 6 * MIB),
        cost_estimate=cost(lines * columns, lines * columns * 6),
        name="round_block",
    )(total)


def first_near_kernel(n_row, ids, dense, *refs):
    pieces = refs[: n_row // 2]
    part, stacked = refs[n_row // 2 :]
    row = ids[0]
    stack(row, 0, pieces, stacked)
    part[...] = dot(dense[:, parity_columns(row & 1, dense.shape[1])], stacked[...])


def first_near(ids, dense, pieces):
    nodes, width = pieces[0].shape
    n_row = 2 * len(pieces)
    return pl.pallas_call(
        functools.partial(first_near_kernel, n_row),
        out_shape=jax.ShapeDtypeStruct((dense.shape[0], width), f32),
        in_specs=[SMEM, VMEM] + [VMEM] * len(pieces),
        out_specs=VMEM,
        scratch_shapes=[pltpu.VMEM((len(pieces) * nodes, width), bf16)],
        compiler_params=params(dense.size * 2 + 6 * MIB),
        cost_estimate=cost(dense.size * width, dense.size),
        name="first_near",
    )(ids, dense, *pieces)


def first_far_kernel(n_row, n_col, ids, dense, part, *refs):
    pieces = refs[: n_row // 2]
    outs, stacked = refs[n_row // 2 : -1], refs[-1]
    nodes = pieces[0].shape[0]
    row, col = ids[0], ids[1]
    stack(row, 1, pieces, stacked)
    columns = parity_columns(1 - (row & 1), dense.shape[1])
    for k in range(n_col):
        lines = pl.ds(pl.multiple_of((col ^ k) * nodes, nodes), nodes)
        outs[k][...] = (part[lines, :] + dot(dense[lines, columns], stacked[...])).astype(bf16)


def first_far(ids, dense, part, pieces, n_col):
    nodes, width = pieces[0].shape
    n_row = 2 * len(pieces)
    return pl.pallas_call(
        functools.partial(first_far_kernel, n_row, n_col),
        out_shape=[jax.ShapeDtypeStruct((nodes, width), bf16)] * n_col,
        in_specs=[SMEM, VMEM, VMEM] + [VMEM] * len(pieces),
        out_specs=[VMEM] * n_col,
        scratch_shapes=[pltpu.VMEM((len(pieces) * nodes, width), bf16)],
        compiler_params=params(dense.size * 2 + 6 * MIB),
        cost_estimate=cost(dense.size * width, dense.size),
        name="first_far",
    )(ids, dense, part, *pieces)


def hidden_pieces(row, start, weight, bias, class_weight, pieces, column, stacked, own):
    nodes = pieces[0].shape[0]
    for k, piece in enumerate(pieces):
        other = start + 2 * k
        pre = dot(piece[...], weight[...]) + bias[...]
        hidden = (pre * (1.0 / (1.0 + jnp.exp(-pre)))).astype(bf16)
        place = pl.ds(pl.multiple_of(((row ^ other) >> 1) * nodes, nodes), nodes)
        column[place, :] = hidden
        if other == 0:
            own[...] = hidden
        high, low = halves(dot(hidden, class_weight[...], ((1,), (1,))))
        stacked[place, :] = jnp.concatenate([high, low], axis=1)


def both_halves(value):
    lanes = value.shape[1] // 2
    return value[:, :lanes] + value[:, lanes:]


def hidden_near_kernel(n_row, ids, dense, weight, bias, class_weight, *refs):
    pieces = refs[: n_row // 2]
    hidden_out, column, part, stacked = refs[n_row // 2 :]
    row = ids[0]
    hidden_pieces(row, 0, weight, bias, class_weight, pieces, column, stacked, hidden_out)
    part[...] = both_halves(dot(dense[:, parity_columns(row & 1, dense.shape[1])], stacked[...]))


def hidden_near(ids, dense, weight, bias, class_weight, pieces):
    nodes = pieces[0].shape[0]
    n_row = 2 * len(pieces)
    width = weight.shape[1]
    lanes = class_weight.shape[0]
    column = n_row * nodes
    return pl.pallas_call(
        functools.partial(hidden_near_kernel, n_row),
        out_shape=[
            jax.ShapeDtypeStruct((nodes, width), bf16),
            jax.ShapeDtypeStruct((column // 2, width), bf16),
            jax.ShapeDtypeStruct((dense.shape[0], lanes), f32),
        ],
        in_specs=[SMEM] + [VMEM] * (4 + len(pieces)),
        out_specs=[VMEM] * 3,
        scratch_shapes=[pltpu.VMEM((column // 2, 2 * lanes), bf16)],
        compiler_params=params(dense.size * 2 + column * width * 8 + 6 * MIB),
        cost_estimate=cost(2 * dense.size * lanes, dense.size, column * width),
        name="hidden_near",
    )(ids, dense, weight, bias, class_weight, *pieces)


def hidden_far_kernel(n_row, n_col, ids, dense, weight, bias, class_weight, code, part, near, *refs):
    pieces = refs[: n_row // 2]
    column, term_out, stacked = refs[n_row // 2 :]
    nodes = pieces[0].shape[0]
    row, col = ids[0], ids[1]
    half = near.shape[0]
    parity = row & 1
    column[pl.ds(pl.multiple_of(parity * half, half), half), :] = near[...]
    other = column.at[pl.ds(pl.multiple_of((1 - parity) * half, half), half), :]
    hidden_pieces(row, 1, weight, bias, class_weight, pieces, other, stacked, None)
    both = dot(dense[:, parity_columns(1 - (row & 1), dense.shape[1])], stacked[...])
    term = (part[...] + both_halves(both)).T[: term_out.shape[0]]
    slice_of = lax.broadcasted_iota(jnp.int32, term.shape, 1) // nodes
    line = lax.broadcasted_iota(jnp.int32, term.shape, 0)
    codes = jnp.where(slice_of == col, jnp.concatenate([code[...]] * n_col, axis=1), 0.0)
    term_out[...] = jnp.where(line == term.shape[0] - 1, codes, term).astype(bf16)


def hidden_far(ids, dense, weight, bias, class_weight, code, part, near, pieces, n_col, lines):
    nodes = pieces[0].shape[0]
    n_row = 2 * len(pieces)
    lanes = class_weight.shape[0]
    return pl.pallas_call(
        functools.partial(hidden_far_kernel, n_row, n_col),
        out_shape=[
            jax.ShapeDtypeStruct((2 * near.shape[0], near.shape[1]), bf16),
            jax.ShapeDtypeStruct((lines, n_col * nodes), bf16),
        ],
        in_specs=[SMEM] + [VMEM] * (7 + len(pieces)),
        out_specs=[VMEM] * 2,
        scratch_shapes=[pltpu.VMEM((near.shape[0], 2 * lanes), bf16)],
        compiler_params=params(dense.size * 2 + near.size * 16 + 6 * MIB),
        cost_estimate=cost(2 * dense.size * lanes, dense.size, 2 * near.size),
        name="hidden_far",
    )(ids, dense, weight, bias, class_weight, code, part, near, *pieces)


def slope_kernel(n_row, ids, weight, bias, *refs):
    pieces = refs[:n_row]
    slope_out, turned_out = refs[n_row:]
    nodes = pieces[0].shape[0]
    row = ids[0]
    for k in range(n_row):
        pre = dot(pieces[k][...], weight[...]) + bias[...]
        sigma = 1.0 / (1.0 + jnp.exp(-pre))
        place = place_of(row, k, n_row, nodes)
        slope_out[place, :] = sigma * (1.0 + pre * (1.0 - sigma))
        turned_out[:, place] = pieces[k][...].T


def slopes(ids, weight, bias, pieces):
    nodes, features = pieces[0].shape
    n_row = len(pieces)
    width = weight.shape[1]
    column = n_row * nodes
    return pl.pallas_call(
        functools.partial(slope_kernel, n_row),
        out_shape=[
            jax.ShapeDtypeStruct((column, width), f32),
            jax.ShapeDtypeStruct((features, column), bf16),
        ],
        in_specs=[SMEM] + [VMEM] * (2 + n_row),
        out_specs=[VMEM] * 2,
        compiler_params=params(column * width * 8 + 4 * MIB),
        cost_estimate=cost(2 * column * features * width, column * width * 4, column * width * 2),
        name="slopes",
    )(ids, weight, bias, *pieces)


def tree_sum(parts):
    parts = [part.astype(f32) for part in parts]
    while len(parts) > 1:
        parts = [parts[k] + parts[k + 1] for k in range(0, len(parts), 2)]
    return parts[0]


def gradient_kernel(n_col, classes, ids, dense, column, slope, turned, class_weight_turned, class_bias, *refs):
    terms = refs[:n_col]
    logits_out, keep_out, send_out, scratch, packed = refs[n_col:]
    lines, nodes_row = terms[0].shape
    nodes = nodes_row // n_col
    features = turned.shape[0]
    width = column.shape[1]
    row, col = ids[0], ids[1]
    total = tree_sum([term[...] for term in terms])
    code = total[lines - 1 :, :]
    live = (code >= MASK_CODE).astype(f32)
    label = (code - MASK_CODE * live).astype(jnp.int32)
    line = lax.broadcasted_iota(jnp.int32, total.shape, 0)
    bias = jnp.broadcast_to(class_bias[...], (8, class_bias.shape[1])).T[:lines, :1]
    logits = jnp.where(line < classes, total + bias, -jnp.inf)
    scratch[...] = logits
    own = pl.ds(pl.multiple_of(col * nodes, nodes), nodes)
    logits_out[...] = scratch[:classes, own]
    top = jnp.max(logits, axis=0, keepdims=True)
    log_total = top + jnp.log(jnp.sum(jnp.exp(logits - top), axis=0, keepdims=True))
    chosen = line == label
    picked = jnp.sum(jnp.where(chosen, logits, 0.0), axis=0, keepdims=True)
    grad = (jnp.exp(logits - log_total) - chosen.astype(f32)) * live
    high, low = halves(grad)
    stacked = jnp.concatenate([high, low], axis=0)
    both = dot(stacked, dense[...])
    back = both[:lines] + both[lines:]
    back_high, back_low = halves(back)
    back_both = jnp.concatenate([back_high, back_low], axis=0)
    class_both = dot(back_both, column[...])
    packed[pl.ds(features, lines), :] = class_both[:lines] + class_both[lines:]
    twice = jnp.concatenate([class_weight_turned[:lines, :]] * 2, axis=0)
    hidden_grad = dot(back_both, twice, ((0,), (0,)))
    pre_grad = hidden_grad * slope[...]
    packed[pl.ds(0, features), :] = dot(turned[...], pre_grad.astype(bf16))
    packed[pl.ds(features + lines - 1, 1), :] = jnp.sum(pre_grad, axis=0, keepdims=True)
    here = (lax.broadcasted_iota(jnp.int32, (8, nodes_row), 1) // nodes == col).astype(f32)
    ours = here.astype(bf16)
    class_sum = dot(ours, high, ((1,), (1,))) + dot(ours, low, ((1,), (1,)))
    class_sum = jnp.concatenate([class_sum, jnp.zeros((8, width - lines), f32)], axis=1)
    loss = jnp.sum((log_total - picked) * live * here[:1])
    members = jnp.sum(live * here[:1])
    lane = lax.broadcasted_iota(jnp.int32, (8, width), 1)
    entry = lax.broadcasted_iota(jnp.int32, (8, width), 0)
    loss = jnp.full((8, width), loss, f32)
    loss_high = loss.astype(bf16).astype(f32)
    loss_middle = (loss - loss_high).astype(bf16).astype(f32)
    loss_low = loss - loss_high - loss_middle
    values = jnp.where(entry == 0, loss_high, jnp.where(entry == 1, loss_middle, loss_low))
    values = jnp.where(entry == 3, members, jnp.where(entry < 3, values, 0.0))
    tail = jnp.where(lane == row * n_col + col, values, 0.0)
    packed[pl.ds(features + lines, 8), :] = class_sum
    packed[pl.ds(features + lines + 8, 8), :] = tail
    part = packed.shape[0] // 2
    core = row & 1
    keep_out[...] = packed[pl.ds(pl.multiple_of(core * part, 8), part), :].astype(keep_out.dtype)
    send_out[...] = packed[pl.ds(pl.multiple_of((1 - core) * part, 8), part), :].astype(send_out.dtype)


def gradients(ids, dense, column, slope, turned, class_weight_turned, class_bias, terms, classes):
    n_col = len(terms)
    lines, nodes_row = terms[0].shape
    width = column.shape[1]
    packed = turned.shape[0] + lines + 16
    return pl.pallas_call(
        functools.partial(gradient_kernel, n_col, classes),
        out_shape=[
            jax.ShapeDtypeStruct((classes, nodes_row // n_col), f32),
            jax.ShapeDtypeStruct((packed // 2, width), WIRE),
            jax.ShapeDtypeStruct((packed // 2, width), WIRE),
        ],
        in_specs=[SMEM] + [VMEM] * (6 + n_col),
        out_specs=[VMEM] * 3,
        scratch_shapes=[
            pltpu.VMEM((lines, nodes_row), f32),
            pltpu.VMEM((packed, width), f32),
        ],
        compiler_params=params(dense.size * 2 + column.size * 16 + 6 * MIB),
        cost_estimate=cost(4 * dense.size * lines, dense.size * 2),
        name="gradients",
    )(ids, dense, column, slope, turned, class_weight_turned, class_bias, *terms)


def finish_kernel(features, lines, classes, ids, mine, other, loss_out, weight_out, bias_out, class_out, class_bias_out, packed):
    part = mine.shape[0]
    core = ids[0] & 1
    packed[pl.ds(pl.multiple_of(core * part, 8), part), :] = mine[...].astype(f32)
    packed[pl.ds(pl.multiple_of((1 - core) * part, 8), part), :] = other[...].astype(f32)
    tail = packed[pl.ds(features + lines + 8, 8), :]
    sums = jnp.sum(tail, axis=1, keepdims=True)
    members = sums[3:4]
    loss_out[...] = (sums[0:1] + sums[1:2] + sums[2:3]) / members
    weight_out[...] = packed[pl.ds(0, features), :] / members
    bias_out[...] = packed[pl.ds(features + lines - 1, 1), :] / members
    class_out[...] = packed[pl.ds(features, classes), :] / members
    class_bias_out[...] = packed[pl.ds(features + lines, 1), :][:, :classes] / members


def finish(ids, mine, other, features, lines, classes):
    part, width = mine.shape
    return pl.pallas_call(
        functools.partial(finish_kernel, features, lines, classes),
        out_shape=[
            jax.ShapeDtypeStruct((1, 1), f32),
            jax.ShapeDtypeStruct((features, width), f32),
            jax.ShapeDtypeStruct((1, width), f32),
            jax.ShapeDtypeStruct((classes, width), f32),
            jax.ShapeDtypeStruct((1, classes), f32),
        ],
        in_specs=[SMEM, VMEM, VMEM],
        out_specs=[VMEM] * 5,
        scratch_shapes=[pltpu.VMEM((2 * part, width), f32)],
        compiler_params=params(4 * MIB),
        name="finish",
    )(ids, mine, other)


def swap(value, axis, mask):
    size = lax.axis_size(axis)
    return lax.ppermute(value, axis, [(k, k ^ mask) for k in range(size)])


def gather_row(value):
    size = lax.axis_size("row")
    even = [value] + [swap(value, "row", k) for k in range(2, size, 2)]
    odd = [swap(even[0], "row", 1)]
    odd += [swap(piece, "row", 1) for piece in even[1:]]
    return even, odd


def sum_over(value, axis, low, high):
    while low < high:
        step = min(2, high - low)
        parts = [value.astype(WIRE)]
        parts += [swap(parts[0], axis, k << low) for k in range(1, 1 << step)]
        value = tree_sum(parts)
        low += step
    return value


def step(
    node_features,
    tile_values,
    tile_rows,
    tile_cols,
    tile_count,
    labels,
    train_mask,
    hidden_weight,
    hidden_bias,
    class_weight,
    class_bias,
):
    nodes, features = node_features.shape
    classes = class_weight.shape[1]
    n_row, n_col = lax.axis_size("row"), lax.axis_size("col")
    row_bits, col_bits = n_row.bit_length() - 1, n_col.bit_length() - 1
    lines = (classes // 16 + 1) * 16
    ids = jnp.stack([lax.axis_index("row"), lax.axis_index("col")]).astype(jnp.int32)
    code = (labels + MASK_CODE * train_mask).astype(f32)[None, :]
    bias = hidden_bias[None, :]
    class_turned = jnp.pad(class_weight.T, ((0, TILE - classes), (0, 0)))
    class_bias_lanes = jnp.pad(class_bias, (0, TILE - classes))[None, :]

    near, far = gather_row(node_features)
    total = collect(
        ids, tile_values[0, 0], tile_rows[0], tile_cols[0], tile_count, n_col * nodes // TILE, n_row * nodes // TILE
    )
    dense = round_block(total, n_col * nodes, n_row * nodes, n_row)
    part = first_near(ids, dense, near)
    terms = first_far(ids, dense, part, far, n_col)
    arrived = [terms[0]] + [swap(terms[k], "col", k) for k in range(1, n_col)]
    first_agg = tree_sum(arrived).astype(bf16)
    near, far = gather_row(first_agg)
    pieces = [piece for pair in zip(near, far) for piece in pair]
    hidden, column_near, part = hidden_near(ids, dense, hidden_weight, bias, class_turned, near)
    column, term = hidden_far(
        ids, dense, hidden_weight, bias, class_turned, code, part, column_near, far, n_col, lines
    )
    class_terms = [term] + [swap(term, "col", k) for k in range(1, n_col)]
    slope, turned = slopes(ids, hidden_weight, bias, pieces)
    logits, keep, send = gradients(
        ids, dense, column, slope, turned, class_turned, class_bias_lanes, class_terms, classes
    )
    part = keep.astype(f32) + swap(send, "row", 1).astype(f32)
    part = sum_over(part, "row", 1, row_bits)
    part = sum_over(part, "col", 0, col_bits)
    mine = part.astype(WIRE)
    other = swap(mine, "row", 1)
    loss, weight_grad, bias_grad, class_grad, class_bias_grad = finish(
        ids, mine, other, features, lines, classes
    )
    return (
        hidden,
        logits,
        loss[0, 0],
        weight_grad,
        bias_grad[0],
        class_grad.T,
        class_bias_grad[0],
    )


def solution(mesh):
    in_specs = (
        P(("row", "col"), None),
        P("row", "col", None, None, None),
        P("row", "col", None),
        P("row", "col", None),
        P("row", "col"),
        P(("row", "col")),
        P(("row", "col")),
        P(),
        P(),
        P(),
        P(),
    )
    out_specs = (P(("row", "col"), None), P(None, ("row", "col")), P(), P(), P(), P(), P())
    return jax.shard_map(step, mesh=mesh, in_specs=in_specs, out_specs=out_specs, check_vma=False)
```

```python
import functools
import math

import jax
import jax.numpy as jnp
from jax import lax
from jax.experimental import pallas as pl
from jax.experimental.pallas import tpu as pltpu
from jax.sharding import PartitionSpec as P


TILE = 128
MASK_CODE = 128
MIB = 1024 * 1024
WIRE = jnp.bfloat16
f32 = jnp.float32
bf16 = jnp.bfloat16


VMEM = pl.BlockSpec(memory_space=pltpu.VMEM)
SMEM = pl.BlockSpec(memory_space=pltpu.SMEM)
HBM = pl.BlockSpec(memory_space=pltpu.HBM)


def params(limit):
    return pltpu.CompilerParams(vmem_limit_bytes=limit)


def cost(flops, moved, transcendentals=0):
    return pl.CostEstimate(flops=flops, bytes_accessed=moved, transcendentals=transcendentals)


def dot(a, b, dims=((1,), (0,))):
    return lax.dot_general(a, b, (dims, ((), ())), preferred_element_type=f32)


def halves(value):
    high = value.astype(bf16)
    return high, (value - high.astype(f32)).astype(bf16)


def collect_kernel(group, depth, tile_cols, ids, count, rows_hbm, cols_hbm, values, total, ring, rows, cols, sem, table_sem):
    slots = values.shape[0]
    groups = slots // group
    spare = total.shape[0] - 1
    tables = [
        pltpu.make_async_copy(source, target, table_sem.at[k])
        for k, (source, target) in enumerate(((rows_hbm, rows), (cols_hbm, cols)))
    ]
    for table in tables:
        table.start()

    def copy(index, slot):
        return pltpu.make_async_copy(
            values.at[pl.ds(index * group, group)], ring.at[slot], sem.at[slot]
        )

    live = count[0, 0]
    groups_live = (live + group - 1) // group
    for slot in range(depth):
        @pl.when(slot < groups_live)
        def _():
            copy(slot, slot).start()

    @pl.loop(0, spare // 4)
    def _(place):
        for k in range(4):
            total[place * 4 + k] = jnp.zeros((TILE, TILE), f32)

    for table in tables:
        table.wait()

    @pl.loop(0, groups_live)
    def _(index):
        slot = lax.rem(index, depth)
        copy(index, slot).wait()
        for k in range(group):
            item = index * group + k
            place = rows[0, item] * tile_cols + cols[0, item]
            place = jnp.where(item < live, place, spare)
            total[place] = total[place] + ring[slot, k].astype(f32)

        if depth < groups:
            @pl.when(index + depth < groups_live)
            def _():
                copy(index + depth, slot).start()


def collect(ids, values, rows, cols, count, tile_rows, tile_cols):
    slots = values.shape[0]
    n_places = tile_rows * tile_cols
    group = math.gcd(slots, 16)
    small = n_places <= 128
    depth = slots // group if small else min(slots // group, 8)
    rows, cols = (pltpu.with_memory_space_constraint(x, pltpu.HBM) for x in (rows, cols))
    return pl.pallas_call(
        functools.partial(collect_kernel, group, depth, tile_cols),
        out_shape=jax.ShapeDtypeStruct((n_places + 1, TILE, TILE), f32),
        in_specs=[SMEM, SMEM, HBM, HBM, HBM],
        out_specs=VMEM,
        scratch_shapes=[
            pltpu.VMEM((depth, group, TILE, TILE), bf16),
            pltpu.SMEM((1, slots), jnp.int32),
            pltpu.SMEM((1, slots), jnp.int32),
            pltpu.SemaphoreType.DMA((depth,)),
            pltpu.SemaphoreType.DMA((2,)),
        ],
        compiler_params=params((44 if small else 56) * MIB),
        cost_estimate=cost(slots * TILE * TILE, slots * TILE * TILE * 2),
        name="collect",
    )(ids, count, rows, cols, values)


def position(row, k, n_row):
    other = row ^ k
    return (other & 1) * (n_row // 2) + (other >> 1)


def place_of(row, k, n_row, nodes):
    return pl.ds(pl.multiple_of(position(row, k, n_row) * nodes, nodes), nodes)


def stack(row, start, pieces, stacked):
    nodes = pieces[0].shape[0]
    for k, piece in enumerate(pieces):
        place = pl.multiple_of(((row ^ (start + 2 * k)) >> 1) * nodes, nodes)
        stacked[pl.ds(place, nodes), :] = piece[...]


def parity_columns(parity, columns):
    return pl.ds(pl.multiple_of(parity * (columns // 2), columns // 2), columns // 2)


def first_near_kernel(n_row, ids, total, *refs):
    pieces = refs[: n_row // 2]
    dense, part, stacked = refs[n_row // 2 :]
    row = ids[0]
    stack(row, 0, pieces, stacked)
    tile_rows = dense.shape[0] // TILE
    tile_cols = dense.shape[1] // TILE
    each = tile_cols // n_row

    @pl.loop(0, tile_rows)
    def _(tile_row):
        lines = pl.ds(pl.multiple_of(tile_row * TILE, TILE), TILE)
        for tile_col in range(tile_cols):
            target = position(tile_col // each, 0, n_row) * each + tile_col % each
            lanes = pl.ds(target * TILE, TILE)
            dense[lines, lanes] = total[tile_row * tile_cols + tile_col].astype(bf16)

    part[...] = dot(dense[:, parity_columns(row & 1, dense.shape[1])], stacked[...])


def first_near(ids, total, pieces, n_col):
    nodes, width = pieces[0].shape
    n_row = 2 * len(pieces)
    size = (n_col * nodes, n_row * nodes)
    return pl.pallas_call(
        functools.partial(first_near_kernel, n_row),
        out_shape=[jax.ShapeDtypeStruct(size, bf16), jax.ShapeDtypeStruct((size[0], width), f32)],
        in_specs=[SMEM, VMEM] + [VMEM] * len(pieces),
        out_specs=[VMEM] * 2,
        scratch_shapes=[pltpu.VMEM((len(pieces) * nodes, width), bf16)],
        compiler_params=params(size[0] * size[1] * 6 + 6 * MIB),
        cost_estimate=cost(size[0] * size[1] * width, size[0] * size[1] * 6),
        name="first_near",
    )(ids, total, *pieces)


def first_far_kernel(n_row, n_col, ids, dense, part, *refs):
    pieces = refs[: n_row // 2]
    outs, stacked = refs[n_row // 2 : -1], refs[-1]
    nodes = pieces[0].shape[0]
    row, col = ids[0], ids[1]
    stack(row, 1, pieces, stacked)
    columns = parity_columns(1 - (row & 1), dense.shape[1])
    for k in range(n_col):
        lines = pl.ds(pl.multiple_of((col ^ k) * nodes, nodes), nodes)
        outs[k][...] = (part[lines, :] + dot(dense[lines, columns], stacked[...])).astype(bf16)


def first_far(ids, dense, part, pieces, n_col):
    nodes, width = pieces[0].shape
    n_row = 2 * len(pieces)
    return pl.pallas_call(
        functools.partial(first_far_kernel, n_row, n_col),
        out_shape=[jax.ShapeDtypeStruct((nodes, width), bf16)] * n_col,
        in_specs=[SMEM, VMEM, VMEM] + [VMEM] * len(pieces),
        out_specs=[VMEM] * n_col,
        scratch_shapes=[pltpu.VMEM((len(pieces) * nodes, width), bf16)],
        compiler_params=params(dense.size * 2 + 6 * MIB),
        cost_estimate=cost(dense.size * width, dense.size),
        name="first_far",
    )(ids, dense, part, *pieces)


def hidden_pieces(row, start, weight, bias, class_weight, pieces, column, stacked, own):
    nodes = pieces[0].shape[0]
    for k, piece in enumerate(pieces):
        other = start + 2 * k
        pre = dot(piece[...], weight[...]) + bias[...]
        hidden = (pre * (1.0 / (1.0 + jnp.exp(-pre)))).astype(bf16)
        place = pl.ds(pl.multiple_of(((row ^ other) >> 1) * nodes, nodes), nodes)
        column[place, :] = hidden
        if other == 0:
            own[...] = hidden
        high, low = halves(dot(hidden, class_weight[...], ((1,), (1,))))
        stacked[place, :] = jnp.concatenate([high, low], axis=1)


def both_halves(value):
    lanes = value.shape[1] // 2
    return value[:, :lanes] + value[:, lanes:]


def hidden_near_kernel(n_row, ids, dense, weight, bias, class_weight, *refs):
    pieces = refs[: n_row // 2]
    hidden_out, column, part, stacked = refs[n_row // 2 :]
    row = ids[0]
    hidden_pieces(row, 0, weight, bias, class_weight, pieces, column, stacked, hidden_out)
    part[...] = both_halves(dot(dense[:, parity_columns(row & 1, dense.shape[1])], stacked[...]))


def hidden_near(ids, dense, weight, bias, class_weight, pieces):
    nodes = pieces[0].shape[0]
    n_row = 2 * len(pieces)
    width = weight.shape[1]
    lanes = class_weight.shape[0]
    column = n_row * nodes
    return pl.pallas_call(
        functools.partial(hidden_near_kernel, n_row),
        out_shape=[
            jax.ShapeDtypeStruct((nodes, width), bf16),
            jax.ShapeDtypeStruct((column // 2, width), bf16),
            jax.ShapeDtypeStruct((dense.shape[0], lanes), f32),
        ],
        in_specs=[SMEM] + [VMEM] * (4 + len(pieces)),
        out_specs=[VMEM] * 3,
        scratch_shapes=[pltpu.VMEM((column // 2, 2 * lanes), bf16)],
        compiler_params=params(dense.size * 2 + column * width * 8 + 6 * MIB),
        cost_estimate=cost(2 * dense.size * lanes, dense.size, column * width),
        name="hidden_near",
    )(ids, dense, weight, bias, class_weight, *pieces)


def hidden_far_kernel(n_row, n_col, ids, dense, weight, bias, class_weight, code, part, near, *refs):
    pieces = refs[: n_row // 2]
    column, term_out, stacked = refs[n_row // 2 :]
    nodes = pieces[0].shape[0]
    row, col = ids[0], ids[1]
    half = near.shape[0]
    parity = row & 1
    column[pl.ds(pl.multiple_of(parity * half, half), half), :] = near[...]
    other = column.at[pl.ds(pl.multiple_of((1 - parity) * half, half), half), :]
    hidden_pieces(row, 1, weight, bias, class_weight, pieces, other, stacked, None)
    both = dot(dense[:, parity_columns(1 - (row & 1), dense.shape[1])], stacked[...])
    term = (part[...] + both_halves(both)).T[: term_out.shape[0]]
    slice_of = lax.broadcasted_iota(jnp.int32, term.shape, 1) // nodes
    line = lax.broadcasted_iota(jnp.int32, term.shape, 0)
    codes = jnp.where(slice_of == col, jnp.concatenate([code[...]] * n_col, axis=1), 0.0)
    term_out[...] = jnp.where(line == term.shape[0] - 1, codes, term).astype(bf16)


def hidden_far(ids, dense, weight, bias, class_weight, code, part, near, pieces, n_col, lines):
    nodes = pieces[0].shape[0]
    n_row = 2 * len(pieces)
    lanes = class_weight.shape[0]
    return pl.pallas_call(
        functools.partial(hidden_far_kernel, n_row, n_col),
        out_shape=[
            jax.ShapeDtypeStruct((2 * near.shape[0], near.shape[1]), bf16),
            jax.ShapeDtypeStruct((lines, n_col * nodes), bf16),
        ],
        in_specs=[SMEM] + [VMEM] * (7 + len(pieces)),
        out_specs=[VMEM] * 2,
        scratch_shapes=[pltpu.VMEM((near.shape[0], 2 * lanes), bf16)],
        compiler_params=params(dense.size * 2 + near.size * 16 + 6 * MIB),
        cost_estimate=cost(2 * dense.size * lanes, dense.size, 2 * near.size),
        name="hidden_far",
    )(ids, dense, weight, bias, class_weight, code, part, near, *pieces)


def slope_kernel(n_row, ids, weight, bias, *refs):
    pieces = refs[:n_row]
    slope_out, turned_out = refs[n_row:]
    nodes = pieces[0].shape[0]
    row = ids[0]
    for k in range(n_row):
        pre = dot(pieces[k][...], weight[...]) + bias[...]
        sigma = 1.0 / (1.0 + jnp.exp(-pre))
        place = place_of(row, k, n_row, nodes)
        slope_out[place, :] = sigma * (1.0 + pre * (1.0 - sigma))
        turned_out[:, place] = pieces[k][...].T


def slopes(ids, weight, bias, pieces):
    nodes, features = pieces[0].shape
    n_row = len(pieces)
    width = weight.shape[1]
    column = n_row * nodes
    return pl.pallas_call(
        functools.partial(slope_kernel, n_row),
        out_shape=[
            jax.ShapeDtypeStruct((column, width), f32),
            jax.ShapeDtypeStruct((features, column), bf16),
        ],
        in_specs=[SMEM] + [VMEM] * (2 + n_row),
        out_specs=[VMEM] * 2,
        compiler_params=params(column * width * 8 + 4 * MIB),
        cost_estimate=cost(2 * column * features * width, column * width * 4, column * width * 2),
        name="slopes",
    )(ids, weight, bias, *pieces)


def tree_sum(parts):
    parts = [part.astype(f32) for part in parts]
    while len(parts) > 1:
        parts = [parts[k] + parts[k + 1] for k in range(0, len(parts), 2)]
    return parts[0]


def gradient_kernel(n_col, classes, ids, dense, column, slope, turned, class_weight_turned, class_bias, *refs):
    terms = refs[:n_col]
    logits_out, keep_out, send_out, scratch, packed = refs[n_col:]
    lines, nodes_row = terms[0].shape
    nodes = nodes_row // n_col
    features = turned.shape[0]
    width = column.shape[1]
    row, col = ids[0], ids[1]
    total = tree_sum([term[...] for term in terms])
    code = total[lines - 1 :, :]
    live = (code >= MASK_CODE).astype(f32)
    label = (code - MASK_CODE * live).astype(jnp.int32)
    line = lax.broadcasted_iota(jnp.int32, total.shape, 0)
    bias = jnp.broadcast_to(class_bias[...], (8, class_bias.shape[1])).T[:lines, :1]
    logits = jnp.where(line < classes, total + bias, -jnp.inf)
    scratch[...] = logits
    own = pl.ds(pl.multiple_of(col * nodes, nodes), nodes)
    logits_out[...] = scratch[:classes, own]
    top = jnp.max(logits, axis=0, keepdims=True)
    log_total = top + jnp.log(jnp.sum(jnp.exp(logits - top), axis=0, keepdims=True))
    chosen = line == label
    picked = jnp.sum(jnp.where(chosen, logits, 0.0), axis=0, keepdims=True)
    grad = (jnp.exp(logits - log_total) - chosen.astype(f32)) * live
    high, low = halves(grad)
    stacked = jnp.concatenate([high, low], axis=0)
    both = dot(stacked, dense[...])
    back = both[:lines] + both[lines:]
    back_high, back_low = halves(back)
    back_both = jnp.concatenate([back_high, back_low], axis=0)
    class_both = dot(back_both, column[...])
    packed[pl.ds(features, lines), :] = class_both[:lines] + class_both[lines:]
    twice = jnp.concatenate([class_weight_turned[:lines, :]] * 2, axis=0)
    hidden_grad = dot(back_both, twice, ((0,), (0,)))
    pre_grad = hidden_grad * slope[...]
    packed[pl.ds(0, features), :] = dot(turned[...], pre_grad.astype(bf16))
    packed[pl.ds(features + lines - 1, 1), :] = jnp.sum(pre_grad, axis=0, keepdims=True)
    here = (lax.broadcasted_iota(jnp.int32, (8, nodes_row), 1) // nodes == col).astype(f32)
    ours = here.astype(bf16)
    class_sum = dot(ours, high, ((1,), (1,))) + dot(ours, low, ((1,), (1,)))
    class_sum = jnp.concatenate([class_sum, jnp.zeros((8, width - lines), f32)], axis=1)
    loss = jnp.sum((log_total - picked) * live * here[:1])
    members = jnp.sum(live * here[:1])
    lane = lax.broadcasted_iota(jnp.int32, (8, width), 1)
    entry = lax.broadcasted_iota(jnp.int32, (8, width), 0)
    loss = jnp.full((8, width), loss, f32)
    loss_high = loss.astype(bf16).astype(f32)
    loss_middle = (loss - loss_high).astype(bf16).astype(f32)
    loss_low = loss - loss_high - loss_middle
    values = jnp.where(entry == 0, loss_high, jnp.where(entry == 1, loss_middle, loss_low))
    values = jnp.where(entry == 3, members, jnp.where(entry < 3, values, 0.0))
    tail = jnp.where(lane == row * n_col + col, values, 0.0)
    packed[pl.ds(features + lines, 8), :] = class_sum
    packed[pl.ds(features + lines + 8, 8), :] = tail
    part = packed.shape[0] // 2
    core = row & 1
    keep_out[...] = packed[pl.ds(pl.multiple_of(core * part, 8), part), :].astype(keep_out.dtype)
    send_out[...] = packed[pl.ds(pl.multiple_of((1 - core) * part, 8), part), :].astype(send_out.dtype)


def gradients(ids, dense, column, slope, turned, class_weight_turned, class_bias, terms, classes):
    n_col = len(terms)
    lines, nodes_row = terms[0].shape
    width = column.shape[1]
    packed = turned.shape[0] + lines + 16
    return pl.pallas_call(
        functools.partial(gradient_kernel, n_col, classes),
        out_shape=[
            jax.ShapeDtypeStruct((classes, nodes_row // n_col), f32),
            jax.ShapeDtypeStruct((packed // 2, width), WIRE),
            jax.ShapeDtypeStruct((packed // 2, width), WIRE),
        ],
        in_specs=[SMEM] + [VMEM] * (6 + n_col),
        out_specs=[VMEM] * 3,
        scratch_shapes=[
            pltpu.VMEM((lines, nodes_row), f32),
            pltpu.VMEM((packed, width), f32),
        ],
        compiler_params=params(dense.size * 2 + column.size * 16 + 6 * MIB),
        cost_estimate=cost(4 * dense.size * lines, dense.size * 2),
        name="gradients",
    )(ids, dense, column, slope, turned, class_weight_turned, class_bias, *terms)


def finish_kernel(features, lines, classes, ids, mine, other, loss_out, weight_out, bias_out, class_out, class_bias_out, packed):
    part = mine.shape[0]
    core = ids[0] & 1
    packed[pl.ds(pl.multiple_of(core * part, 8), part), :] = mine[...].astype(f32)
    packed[pl.ds(pl.multiple_of((1 - core) * part, 8), part), :] = other[...].astype(f32)
    tail = packed[pl.ds(features + lines + 8, 8), :]
    sums = jnp.sum(tail, axis=1, keepdims=True)
    members = sums[3:4]
    loss_out[...] = (sums[0:1] + sums[1:2] + sums[2:3]) / members
    weight_out[...] = packed[pl.ds(0, features), :] / members
    bias_out[...] = packed[pl.ds(features + lines - 1, 1), :] / members
    class_out[...] = packed[pl.ds(features, classes), :] / members
    class_bias_out[...] = packed[pl.ds(features + lines, 1), :][:, :classes] / members


def finish(ids, mine, other, features, lines, classes):
    part, width = mine.shape
    return pl.pallas_call(
        functools.partial(finish_kernel, features, lines, classes),
        out_shape=[
            jax.ShapeDtypeStruct((1, 1), f32),
            jax.ShapeDtypeStruct((features, width), f32),
            jax.ShapeDtypeStruct((1, width), f32),
            jax.ShapeDtypeStruct((classes, width), f32),
            jax.ShapeDtypeStruct((1, classes), f32),
        ],
        in_specs=[SMEM, VMEM, VMEM],
        out_specs=[VMEM] * 5,
        scratch_shapes=[pltpu.VMEM((2 * part, width), f32)],
        compiler_params=params(4 * MIB),
        name="finish",
    )(ids, mine, other)


def swap(value, axis, mask):
    size = lax.axis_size(axis)
    return lax.ppermute(value, axis, [(k, k ^ mask) for k in range(size)])


def gather_row(value):
    size = lax.axis_size("row")
    even = [value] + [swap(value, "row", k) for k in range(2, size, 2)]
    odd = [swap(even[0], "row", 1)]
    odd += [swap(piece, "row", 1) for piece in even[1:]]
    return even, odd


def sum_over(value, axis, low, high):
    while low < high:
        step = min(2, high - low)
        parts = [value.astype(WIRE)]
        parts += [swap(parts[0], axis, k << low) for k in range(1, 1 << step)]
        value = tree_sum(parts)
        low += step
    return value


def sum_over_chips(value):
    size = lax.axis_size("row")
    masks = [1 << bit for bit in range(1, size.bit_length() - 1)]
    for up, down in zip(masks, masks[::-1]):
        mine = value.astype(WIRE)
        other = lax.ppermute(mine, "row", [(k, k ^ (down if k & 1 else up)) for k in range(size)])
        value = mine.astype(f32) + other.astype(f32)
    return value


def step(
    node_features,
    tile_values,
    tile_rows,
    tile_cols,
    tile_count,
    labels,
    train_mask,
    hidden_weight,
    hidden_bias,
    class_weight,
    class_bias,
):
    nodes, features = node_features.shape
    classes = class_weight.shape[1]
    n_row, n_col = lax.axis_size("row"), lax.axis_size("col")
    col_bits = n_col.bit_length() - 1
    lines = (classes // 16 + 1) * 16
    ids = jnp.stack([lax.axis_index("row"), lax.axis_index("col")]).astype(jnp.int32)
    code = (labels + MASK_CODE * train_mask).astype(f32)[None, :]
    bias = hidden_bias[None, :]
    class_turned = jnp.pad(class_weight.T, ((0, TILE - classes), (0, 0)))
    class_bias_lanes = jnp.pad(class_bias, (0, TILE - classes))[None, :]

    near, far = gather_row(node_features)
    total = collect(
        ids, tile_values[0, 0], tile_rows[0], tile_cols[0], tile_count, n_col * nodes // TILE, n_row * nodes // TILE
    )
    dense, part = first_near(ids, total, near, n_col)
    terms = first_far(ids, dense, part, far, n_col)
    arrived = [terms[0]] + [swap(terms[k], "col", k) for k in range(1, n_col)]
    first_agg = tree_sum(arrived).astype(bf16)
    near, far = gather_row(first_agg)
    pieces = [piece for pair in zip(near, far) for piece in pair]
    hidden, column_near, part = hidden_near(ids, dense, hidden_weight, bias, class_turned, near)
    column, term = hidden_far(
        ids, dense, hidden_weight, bias, class_turned, code, part, column_near, far, n_col, lines
    )
    class_terms = [term] + [swap(term, "col", k) for k in range(1, n_col)]
    slope, turned = slopes(ids, hidden_weight, bias, pieces)
    logits, keep, send = gradients(
        ids, dense, column, slope, turned, class_turned, class_bias_lanes, class_terms, classes
    )
    part = keep.astype(f32) + swap(send, "row", 1).astype(f32)
    part = sum_over_chips(part)
    part = sum_over(part, "col", 0, col_bits)
    mine = part.astype(WIRE)
    other = swap(mine, "row", 1)
    loss, weight_grad, bias_grad, class_grad, class_bias_grad = finish(
        ids, mine, other, features, lines, classes
    )
    return (
        hidden,
        logits,
        loss[0, 0],
        weight_grad,
        bias_grad[0],
        class_grad.T,
        class_bias_grad[0],
    )


def solution(mesh):
    in_specs = (
        P(("row", "col"), None),
        P("row", "col", None, None, None),
        P("row", "col", None),
        P("row", "col", None),
        P("row", "col"),
        P(("row", "col")),
        P(("row", "col")),
        P(),
        P(),
        P(),
        P(),
    )
    out_specs = (P(("row", "col"), None), P(None, ("row", "col")), P(), P(), P(), P(), P())
    return jax.shard_map(step, mesh=mesh, in_specs=in_specs, out_specs=out_specs, check_vma=False)
```

```python
import functools
import math

import jax
import jax.numpy as jnp
from jax import lax
from jax.experimental import pallas as pl
from jax.experimental.pallas import tpu as pltpu
from jax.sharding import PartitionSpec as P


TILE = 128
MASK_CODE = 128
MIB = 1024 * 1024
WIRE = jnp.bfloat16
f32 = jnp.float32
bf16 = jnp.bfloat16


VMEM = pl.BlockSpec(memory_space=pltpu.VMEM)
SMEM = pl.BlockSpec(memory_space=pltpu.SMEM)
HBM = pl.BlockSpec(memory_space=pltpu.HBM)


def params(limit):
    return pltpu.CompilerParams(vmem_limit_bytes=limit)


def cost(flops, moved, transcendentals=0):
    return pl.CostEstimate(flops=flops, bytes_accessed=moved, transcendentals=transcendentals)


def dot(a, b, dims=((1,), (0,))):
    return lax.dot_general(a, b, (dims, ((), ())), preferred_element_type=f32)


def halves(value):
    high = value.astype(bf16)
    return high, (value - high.astype(f32)).astype(bf16)


def collect_kernel(group, depth, tile_cols, count, rows_hbm, cols_hbm, values, total, ring, rows, cols, sem, table_sem):
    slots = values.shape[0]
    groups = slots // group
    spare = total.shape[0] - 1
    tables = [
        pltpu.make_async_copy(source, target, table_sem.at[k])
        for k, (source, target) in enumerate(((rows_hbm, rows), (cols_hbm, cols)))
    ]
    for table in tables:
        table.start()

    def copy(index, slot):
        return pltpu.make_async_copy(
            values.at[pl.ds(index * group, group)], ring.at[slot], sem.at[slot]
        )

    live = count[0, 0]
    groups_live = (live + group - 1) // group
    for slot in range(depth):
        @pl.when(slot < groups_live)
        def _():
            copy(slot, slot).start()

    @pl.loop(0, spare // 4)
    def _(place):
        for k in range(4):
            total[place * 4 + k] = jnp.zeros((TILE, TILE), f32)

    for table in tables:
        table.wait()

    @pl.loop(0, groups_live)
    def _(index):
        slot = lax.rem(index, depth)
        copy(index, slot).wait()
        for k in range(group):
            item = index * group + k
            place = rows[0, item] * tile_cols + cols[0, item]
            place = jnp.where(item < live, place, spare)
            total[place] = total[place] + ring[slot, k].astype(f32)

        if depth < groups:
            @pl.when(index + depth < groups_live)
            def _():
                copy(index + depth, slot).start()


def collect(values, rows, cols, count, tile_rows, tile_cols):
    slots = values.shape[0]
    n_places = tile_rows * tile_cols
    group = math.gcd(slots, 16)
    small = n_places <= 128
    depth = slots // group if small else min(slots // group, 8)
    rows, cols = (pltpu.with_memory_space_constraint(x, pltpu.HBM) for x in (rows, cols))
    return pl.pallas_call(
        functools.partial(collect_kernel, group, depth, tile_cols),
        out_shape=jax.ShapeDtypeStruct((n_places + 1, TILE, TILE), f32),
        in_specs=[SMEM, HBM, HBM, HBM],
        out_specs=VMEM,
        scratch_shapes=[
            pltpu.VMEM((depth, group, TILE, TILE), bf16),
            pltpu.SMEM((1, slots), jnp.int32),
            pltpu.SMEM((1, slots), jnp.int32),
            pltpu.SemaphoreType.DMA((depth,)),
            pltpu.SemaphoreType.DMA((2,)),
        ],
        compiler_params=params((44 if small else 56) * MIB),
        cost_estimate=cost(slots * TILE * TILE, slots * TILE * TILE * 2),
        name="collect",
    )(count, rows, cols, values)


def position(row, k, n_row):
    other = row ^ k
    return (other & 1) * (n_row // 2) + (other >> 1)


def place_of(row, k, n_row, nodes):
    return pl.ds(pl.multiple_of(position(row, k, n_row) * nodes, nodes), nodes)


def stack(row, start, pieces, stacked):
    nodes = pieces[0].shape[0]
    for k, piece in enumerate(pieces):
        place = pl.multiple_of(((row ^ (start + 2 * k)) >> 1) * nodes, nodes)
        stacked[pl.ds(place, nodes), :] = piece[...]


def parity_columns(parity, columns):
    return pl.ds(pl.multiple_of(parity * (columns // 2), columns // 2), columns // 2)


def first_near_kernel(n_row, ids, total, *refs):
    pieces = refs[: n_row // 2]
    dense, part, stacked = refs[n_row // 2 :]
    row = ids[0]
    stack(row, 0, pieces, stacked)
    tile_rows = dense.shape[0] // TILE
    tile_cols = dense.shape[1] // TILE
    each = tile_cols // n_row

    @pl.loop(0, tile_rows)
    def _(tile_row):
        lines = pl.ds(pl.multiple_of(tile_row * TILE, TILE), TILE)
        for tile_col in range(tile_cols):
            target = position(tile_col // each, 0, n_row) * each + tile_col % each
            lanes = pl.ds(target * TILE, TILE)
            dense[lines, lanes] = total[tile_row * tile_cols + tile_col].astype(bf16)

    part[...] = dot(dense[:, parity_columns(row & 1, dense.shape[1])], stacked[...])


def first_near(ids, total, pieces, n_col):
    nodes, width = pieces[0].shape
    n_row = 2 * len(pieces)
    size = (n_col * nodes, n_row * nodes)
    return pl.pallas_call(
        functools.partial(first_near_kernel, n_row),
        out_shape=[jax.ShapeDtypeStruct(size, bf16), jax.ShapeDtypeStruct((size[0], width), f32)],
        in_specs=[SMEM, VMEM] + [VMEM] * len(pieces),
        out_specs=[VMEM] * 2,
        scratch_shapes=[pltpu.VMEM((len(pieces) * nodes, width), bf16)],
        compiler_params=params(size[0] * size[1] * 6 + 6 * MIB),
        cost_estimate=cost(size[0] * size[1] * width, size[0] * size[1] * 6),
        name="first_near",
    )(ids, total, *pieces)


def first_far_kernel(n_row, n_col, ids, dense, part, *refs):
    pieces = refs[: n_row // 2]
    outs, stacked = refs[n_row // 2 : -1], refs[-1]
    nodes = pieces[0].shape[0]
    row, col = ids[0], ids[1]
    stack(row, 1, pieces, stacked)
    columns = parity_columns(1 - (row & 1), dense.shape[1])
    for k in range(n_col):
        lines = pl.ds(pl.multiple_of((col ^ k) * nodes, nodes), nodes)
        outs[k][...] = (part[lines, :] + dot(dense[lines, columns], stacked[...])).astype(bf16)


def first_far(ids, dense, part, pieces, n_col):
    nodes, width = pieces[0].shape
    n_row = 2 * len(pieces)
    return pl.pallas_call(
        functools.partial(first_far_kernel, n_row, n_col),
        out_shape=[jax.ShapeDtypeStruct((nodes, width), bf16)] * n_col,
        in_specs=[SMEM, VMEM, VMEM] + [VMEM] * len(pieces),
        out_specs=[VMEM] * n_col,
        scratch_shapes=[pltpu.VMEM((len(pieces) * nodes, width), bf16)],
        compiler_params=params(dense.size * 2 + 6 * MIB),
        cost_estimate=cost(dense.size * width, dense.size),
        name="first_far",
    )(ids, dense, part, *pieces)


def hidden_kernel(n_row, n_col, ids, dense, weight, bias, class_weight, code, *refs):
    pieces = refs[:n_row]
    hidden_out, column_out, term_out, stacked = refs[n_row:]
    nodes = pieces[0].shape[0]
    row, col = ids[0], ids[1]
    for k in range(n_row):
        pre = dot(pieces[k][...], weight[...]) + bias[...]
        hidden = (pre * (1.0 / (1.0 + jnp.exp(-pre)))).astype(bf16)
        place = place_of(row, k, n_row, nodes)
        column_out[place, :] = hidden
        if k == 0:
            hidden_out[...] = hidden
        high, low = halves(dot(hidden, class_weight[...], ((1,), (1,))))
        stacked[place, :] = jnp.concatenate([high, low], axis=1)
    both = dot(dense[...], stacked[...])
    lanes = both.shape[1] // 2
    term = (both[:, :lanes] + both[:, lanes:]).T[: term_out.shape[0]]
    slice_of = lax.broadcasted_iota(jnp.int32, term.shape, 1) // nodes
    line = lax.broadcasted_iota(jnp.int32, term.shape, 0)
    codes = jnp.where(slice_of == col, jnp.concatenate([code[...]] * n_col, axis=1), 0.0)
    term_out[...] = jnp.where(line == term.shape[0] - 1, codes, term).astype(bf16)


def hidden_terms(ids, dense, weight, bias, class_weight, code, pieces, n_col, lines):
    nodes = pieces[0].shape[0]
    n_row = len(pieces)
    width = weight.shape[1]
    lanes = class_weight.shape[0]
    column = n_row * nodes
    return pl.pallas_call(
        functools.partial(hidden_kernel, n_row, n_col),
        out_shape=[
            jax.ShapeDtypeStruct((nodes, width), bf16),
            jax.ShapeDtypeStruct((column, width), bf16),
            jax.ShapeDtypeStruct((lines, n_col * nodes), bf16),
        ],
        in_specs=[SMEM] + [VMEM] * (5 + n_row),
        out_specs=[VMEM] * 3,
        scratch_shapes=[pltpu.VMEM((column, 2 * lanes), bf16)],
        compiler_params=params(dense.size * 2 + column * width * 8 + 6 * MIB),
        cost_estimate=cost(4 * dense.size * lanes, dense.size * 2, column * width * 2),
        name="hidden_terms",
    )(ids, dense, weight, bias, class_weight, code, *pieces)


def slope_kernel(n_row, ids, weight, bias, *refs):
    pieces = refs[:n_row]
    slope_out, turned_out = refs[n_row:]
    nodes = pieces[0].shape[0]
    row = ids[0]
    for k in range(n_row):
        pre = dot(pieces[k][...], weight[...]) + bias[...]
        sigma = 1.0 / (1.0 + jnp.exp(-pre))
        place = place_of(row, k, n_row, nodes)
        slope_out[place, :] = sigma * (1.0 + pre * (1.0 - sigma))
        turned_out[:, place] = pieces[k][...].T


def slopes(ids, weight, bias, pieces):
    nodes, features = pieces[0].shape
    n_row = len(pieces)
    width = weight.shape[1]
    column = n_row * nodes
    return pl.pallas_call(
        functools.partial(slope_kernel, n_row),
        out_shape=[
            jax.ShapeDtypeStruct((column, width), f32),
            jax.ShapeDtypeStruct((features, column), bf16),
        ],
        in_specs=[SMEM] + [VMEM] * (2 + n_row),
        out_specs=[VMEM] * 2,
        compiler_params=params(column * width * 8 + 4 * MIB),
        cost_estimate=cost(2 * column * features * width, column * width * 4, column * width * 2),
        name="slopes",
    )(ids, weight, bias, *pieces)


def tree_sum(parts):
    parts = [part.astype(f32) for part in parts]
    while len(parts) > 1:
        parts = [parts[k] + parts[k + 1] for k in range(0, len(parts), 2)]
    return parts[0]


def gradient_kernel(n_col, classes, ids, dense, column, slope, turned, class_weight_turned, class_bias, *refs):
    terms = refs[:n_col]
    logits_out, keep_out, send_out, scratch, packed = refs[n_col:]
    lines, nodes_row = terms[0].shape
    nodes = nodes_row // n_col
    features = turned.shape[0]
    width = column.shape[1]
    row, col = ids[0], ids[1]
    total = tree_sum([term[...] for term in terms])
    code = total[lines - 1 :, :]
    live = (code >= MASK_CODE).astype(f32)
    label = (code - MASK_CODE * live).astype(jnp.int32)
    line = lax.broadcasted_iota(jnp.int32, total.shape, 0)
    bias = jnp.broadcast_to(class_bias[...], (8, class_bias.shape[1])).T[:lines, :1]
    logits = jnp.where(line < classes, total + bias, -jnp.inf)
    scratch[...] = logits
    own = pl.ds(pl.multiple_of(col * nodes, nodes), nodes)
    logits_out[...] = scratch[:classes, own]
    top = jnp.max(logits, axis=0, keepdims=True)
    log_total = top + jnp.log(jnp.sum(jnp.exp(logits - top), axis=0, keepdims=True))
    chosen = line == label
    picked = jnp.sum(jnp.where(chosen, logits, 0.0), axis=0, keepdims=True)
    grad = (jnp.exp(logits - log_total) - chosen.astype(f32)) * live
    high, low = halves(grad)
    stacked = jnp.concatenate([high, low], axis=0)
    both = dot(stacked, dense[...])
    back = both[:lines] + both[lines:]
    back_high, back_low = halves(back)
    back_both = jnp.concatenate([back_high, back_low], axis=0)
    class_both = dot(back_both, column[...])
    packed[pl.ds(features, lines), :] = class_both[:lines] + class_both[lines:]
    twice = jnp.concatenate([class_weight_turned[:lines, :]] * 2, axis=0)
    hidden_grad = dot(back_both, twice, ((0,), (0,)))
    pre_grad = hidden_grad * slope[...]
    packed[pl.ds(0, features), :] = dot(turned[...], pre_grad.astype(bf16))
    packed[pl.ds(features + lines - 1, 1), :] = jnp.sum(pre_grad, axis=0, keepdims=True)
    here = (lax.broadcasted_iota(jnp.int32, (8, nodes_row), 1) // nodes == col).astype(f32)
    ours = here.astype(bf16)
    class_sum = dot(ours, high, ((1,), (1,))) + dot(ours, low, ((1,), (1,)))
    class_sum = jnp.concatenate([class_sum, jnp.zeros((8, width - lines), f32)], axis=1)
    loss = jnp.sum((log_total - picked) * live * here[:1])
    members = jnp.sum(live * here[:1])
    lane = lax.broadcasted_iota(jnp.int32, (8, width), 1)
    entry = lax.broadcasted_iota(jnp.int32, (8, width), 0)
    loss = jnp.full((8, width), loss, f32)
    loss_high = loss.astype(bf16).astype(f32)
    loss_middle = (loss - loss_high).astype(bf16).astype(f32)
    loss_low = loss - loss_high - loss_middle
    values = jnp.where(entry == 0, loss_high, jnp.where(entry == 1, loss_middle, loss_low))
    values = jnp.where(entry == 3, members, jnp.where(entry < 3, values, 0.0))
    tail = jnp.where(lane == row * n_col + col, values, 0.0)
    packed[pl.ds(features + lines, 8), :] = class_sum
    packed[pl.ds(features + lines + 8, 8), :] = tail
    part = packed.shape[0] // 2
    core = row & 1
    keep_out[...] = packed[pl.ds(pl.multiple_of(core * part, 8), part), :].astype(keep_out.dtype)
    send_out[...] = packed[pl.ds(pl.multiple_of((1 - core) * part, 8), part), :].astype(send_out.dtype)


def gradients(ids, dense, column, slope, turned, class_weight_turned, class_bias, terms, classes):
    n_col = len(terms)
    lines, nodes_row = terms[0].shape
    width = column.shape[1]
    packed = turned.shape[0] + lines + 16
    return pl.pallas_call(
        functools.partial(gradient_kernel, n_col, classes),
        out_shape=[
            jax.ShapeDtypeStruct((classes, nodes_row // n_col), f32),
            jax.ShapeDtypeStruct((packed // 2, width), WIRE),
            jax.ShapeDtypeStruct((packed // 2, width), WIRE),
        ],
        in_specs=[SMEM] + [VMEM] * (6 + n_col),
        out_specs=[VMEM] * 3,
        scratch_shapes=[
            pltpu.VMEM((lines, nodes_row), f32),
            pltpu.VMEM((packed, width), f32),
        ],
        compiler_params=params(dense.size * 2 + column.size * 16 + 6 * MIB),
        cost_estimate=cost(4 * dense.size * lines, dense.size * 2),
        name="gradients",
    )(ids, dense, column, slope, turned, class_weight_turned, class_bias, *terms)


def finish_kernel(features, lines, classes, ids, mine, other, loss_out, weight_out, bias_out, class_out, class_bias_out, packed):
    part = mine.shape[0]
    core = ids[0] & 1
    packed[pl.ds(pl.multiple_of(core * part, 8), part), :] = mine[...].astype(f32)
    packed[pl.ds(pl.multiple_of((1 - core) * part, 8), part), :] = other[...].astype(f32)
    tail = packed[pl.ds(features + lines + 8, 8), :]
    sums = jnp.sum(tail, axis=1, keepdims=True)
    members = sums[3:4]
    loss_out[...] = (sums[0:1] + sums[1:2] + sums[2:3]) / members
    weight_out[...] = packed[pl.ds(0, features), :] / members
    bias_out[...] = packed[pl.ds(features + lines - 1, 1), :] / members
    class_out[...] = packed[pl.ds(features, classes), :] / members
    class_bias_out[...] = packed[pl.ds(features + lines, 1), :][:, :classes] / members


def finish(ids, mine, other, features, lines, classes):
    part, width = mine.shape
    return pl.pallas_call(
        functools.partial(finish_kernel, features, lines, classes),
        out_shape=[
            jax.ShapeDtypeStruct((1, 1), f32),
            jax.ShapeDtypeStruct((features, width), f32),
            jax.ShapeDtypeStruct((1, width), f32),
            jax.ShapeDtypeStruct((classes, width), f32),
            jax.ShapeDtypeStruct((1, classes), f32),
        ],
        in_specs=[SMEM, VMEM, VMEM],
        out_specs=[VMEM] * 5,
        scratch_shapes=[pltpu.VMEM((2 * part, width), f32)],
        compiler_params=params(4 * MIB),
        name="finish",
    )(ids, mine, other)


def swap(value, axis, mask):
    size = lax.axis_size(axis)
    return lax.ppermute(value, axis, [(k, k ^ mask) for k in range(size)])


def gather_row(value):
    size = lax.axis_size("row")
    even = [value] + [swap(value, "row", k) for k in range(2, size, 2)]
    odd = [swap(even[0], "row", 1)]
    odd += [swap(piece, "row", 1) for piece in even[1:]]
    return even, odd


def sum_over(value, axis, low, high):
    while low < high:
        step = min(2, high - low)
        parts = [value.astype(WIRE)]
        parts += [swap(parts[0], axis, k << low) for k in range(1, 1 << step)]
        value = tree_sum(parts)
        low += step
    return value


def step(
    node_features,
    tile_values,
    tile_rows,
    tile_cols,
    tile_count,
    labels,
    train_mask,
    hidden_weight,
    hidden_bias,
    class_weight,
    class_bias,
):
    nodes, features = node_features.shape
    classes = class_weight.shape[1]
    n_row, n_col = lax.axis_size("row"), lax.axis_size("col")
    row_bits, col_bits = n_row.bit_length() - 1, n_col.bit_length() - 1
    lines = (classes // 16 + 1) * 16
    ids = jnp.stack([lax.axis_index("row"), lax.axis_index("col")]).astype(jnp.int32)
    code = (labels + MASK_CODE * train_mask).astype(f32)[None, :]
    bias = hidden_bias[None, :]
    class_turned = jnp.pad(class_weight.T, ((0, TILE - classes), (0, 0)))
    class_bias_lanes = jnp.pad(class_bias, (0, TILE - classes))[None, :]

    near, far = gather_row(node_features)
    total = collect(
        tile_values[0, 0], tile_rows[0], tile_cols[0], tile_count, n_col * nodes // TILE, n_row * nodes // TILE
    )
    dense, part = first_near(ids, total, near, n_col)
    terms = first_far(ids, dense, part, far, n_col)
    arrived = [terms[0]] + [swap(terms[k], "col", k) for k in range(1, n_col)]
    first_agg = tree_sum(arrived).astype(bf16)
    near, far = gather_row(first_agg)
    pieces = [piece for pair in zip(near, far) for piece in pair]
    hidden, column, term = hidden_terms(
        ids, dense, hidden_weight, bias, class_turned, code, pieces, n_col, lines
    )
    class_terms = [term] + [swap(term, "col", k) for k in range(1, n_col)]
    slope, turned = slopes(ids, hidden_weight, bias, pieces)
    logits, keep, send = gradients(
        ids, dense, column, slope, turned, class_turned, class_bias_lanes, class_terms, classes
    )
    part = keep.astype(f32) + swap(send, "row", 1).astype(f32)
    part = sum_over(part, "row", 1, row_bits)
    part = sum_over(part, "col", 0, col_bits)
    mine = part.astype(WIRE)
    other = swap(mine, "row", 1)
    loss, weight_grad, bias_grad, class_grad, class_bias_grad = finish(
        ids, mine, other, features, lines, classes
    )
    return (
        hidden,
        logits,
        loss[0, 0],
        weight_grad,
        bias_grad[0],
        class_grad.T,
        class_bias_grad[0],
    )


def solution(mesh):
    in_specs = (
        P(("row", "col"), None),
        P("row", "col", None, None, None),
        P("row", "col", None),
        P("row", "col", None),
        P("row", "col"),
        P(("row", "col")),
        P(("row", "col")),
        P(),
        P(),
        P(),
        P(),
    )
    out_specs = (P(("row", "col"), None), P(None, ("row", "col")), P(), P(), P(), P(), P())
    return jax.shard_map(step, mesh=mesh, in_specs=in_specs, out_specs=out_specs, check_vma=False)
```

```python
import functools
import math

import jax
import jax.numpy as jnp
from jax import lax
from jax.experimental import pallas as pl
from jax.experimental.pallas import tpu as pltpu
from jax.sharding import PartitionSpec as P


TILE = 128
MASK_CODE = 128
MIB = 1024 * 1024
WIRE = jnp.bfloat16
f32 = jnp.float32
bf16 = jnp.bfloat16


VMEM = pl.BlockSpec(memory_space=pltpu.VMEM)
SMEM = pl.BlockSpec(memory_space=pltpu.SMEM)
HBM = pl.BlockSpec(memory_space=pltpu.HBM)


def params(limit):
    return pltpu.CompilerParams(vmem_limit_bytes=limit)


def cost(flops, moved, transcendentals=0):
    return pl.CostEstimate(flops=flops, bytes_accessed=moved, transcendentals=transcendentals)


def dot(a, b, dims=((1,), (0,))):
    return lax.dot_general(a, b, (dims, ((), ())), preferred_element_type=f32)


def halves(value):
    high = value.astype(bf16)
    return high, (value - high.astype(f32)).astype(bf16)


def collect_kernel(group, depth, tile_cols, count, rows_hbm, cols_hbm, values, total, ring, rows, cols, sem, table_sem):
    slots = values.shape[0]
    groups = slots // group
    spare = total.shape[0] - 1
    tables = [
        pltpu.make_async_copy(source, target, table_sem.at[k])
        for k, (source, target) in enumerate(((rows_hbm, rows), (cols_hbm, cols)))
    ]
    for table in tables:
        table.start()

    def copy(index, slot):
        return pltpu.make_async_copy(
            values.at[pl.ds(index * group, group)], ring.at[slot], sem.at[slot]
        )

    live = count[0, 0]
    groups_live = (live + group - 1) // group
    for slot in range(depth):
        @pl.when(slot < groups_live)
        def _():
            copy(slot, slot).start()

    @pl.loop(0, spare // 4)
    def _(place):
        for k in range(4):
            total[place * 4 + k] = jnp.zeros((TILE, TILE), f32)

    for table in tables:
        table.wait()

    @pl.loop(0, groups_live)
    def _(index):
        slot = lax.rem(index, depth)
        copy(index, slot).wait()
        for k in range(group):
            item = index * group + k
            place = rows[0, item] * tile_cols + cols[0, item]
            place = jnp.where(item < live, place, spare)
            total[place] = total[place] + ring[slot, k].astype(f32)

        if depth < groups:
            @pl.when(index + depth < groups_live)
            def _():
                copy(index + depth, slot).start()


def collect(values, rows, cols, count, tile_rows, tile_cols):
    slots = values.shape[0]
    n_places = tile_rows * tile_cols
    group = math.gcd(slots, 16)
    small = n_places <= 128
    depth = slots // group if small else min(slots // group, 8)
    rows, cols = (pltpu.with_memory_space_constraint(x, pltpu.HBM) for x in (rows, cols))
    return pl.pallas_call(
        functools.partial(collect_kernel, group, depth, tile_cols),
        out_shape=jax.ShapeDtypeStruct((n_places + 1, TILE, TILE), f32),
        in_specs=[SMEM, HBM, HBM, HBM],
        out_specs=VMEM,
        scratch_shapes=[
            pltpu.VMEM((depth, group, TILE, TILE), bf16),
            pltpu.SMEM((1, slots), jnp.int32),
            pltpu.SMEM((1, slots), jnp.int32),
            pltpu.SemaphoreType.DMA((depth,)),
            pltpu.SemaphoreType.DMA((2,)),
        ],
        compiler_params=params((44 if small else 56) * MIB),
        cost_estimate=cost(slots * TILE * TILE, slots * TILE * TILE * 2),
        name="collect",
    )(count, rows, cols, values)


def position(row, k, n_row):
    other = row ^ k
    return (other & 1) * (n_row // 2) + (other >> 1)


def place_of(row, k, n_row, nodes):
    return pl.ds(pl.multiple_of(position(row, k, n_row) * nodes, nodes), nodes)


def round_kernel(n_row, total, dense):
    tile_rows = dense.shape[0] // TILE
    tile_cols = dense.shape[1] // TILE
    each = tile_cols // n_row

    @pl.loop(0, tile_rows)
    def _(tile_row):
        lines = pl.ds(pl.multiple_of(tile_row * TILE, TILE), TILE)
        for tile_col in range(tile_cols):
            target = position(tile_col // each, 0, n_row) * each + tile_col % each
            lanes = pl.ds(target * TILE, TILE)
            dense[lines, lanes] = total[tile_row * tile_cols + tile_col].astype(bf16)


def round_block(total, lines, columns, n_row):
    return pl.pallas_call(
        functools.partial(round_kernel, n_row),
        out_shape=jax.ShapeDtypeStruct((lines, columns), bf16),
        in_specs=[VMEM],
        out_specs=VMEM,
        compiler_params=params(lines * columns * 6 + 6 * MIB),
        cost_estimate=cost(lines * columns, lines * columns * 6),
        name="round_block",
    )(total)


def first_kernel(n_row, n_col, ids, dense, *refs):
    pieces, outs = refs[:n_row], refs[n_row : n_row + n_col]
    stacked, whole = refs[-2:]
    nodes = pieces[0].shape[0]
    row, col = ids[0], ids[1]
    for k in range(n_row):
        stacked[place_of(row, k, n_row, nodes), :] = pieces[k][...]
    whole[...] = dot(dense[...], stacked[...]).astype(bf16)
    for k in range(n_col):
        outs[k][...] = whole[pl.ds(pl.multiple_of((col ^ k) * nodes, nodes), nodes), :]


def first_terms(ids, dense, pieces, n_col):
    nodes, width = pieces[0].shape
    n_row = len(pieces)
    return pl.pallas_call(
        functools.partial(first_kernel, n_row, n_col),
        out_shape=[jax.ShapeDtypeStruct((nodes, width), bf16)] * n_col,
        in_specs=[SMEM, VMEM] + [VMEM] * n_row,
        out_specs=[VMEM] * n_col,
        scratch_shapes=[
            pltpu.VMEM((n_row * nodes, width), bf16),
            pltpu.VMEM((n_col * nodes, width), bf16),
        ],
        compiler_params=params(dense.size * 2 + 6 * MIB),
        cost_estimate=cost(2 * dense.size * width, dense.size * 2),
        name="first_terms",
    )(ids, dense, *pieces)


def hidden_kernel(n_row, n_col, ids, dense, weight, bias, class_weight, code, *refs):
    pieces = refs[:n_row]
    hidden_out, column_out, term_out, stacked, gathered = refs[n_row:]
    nodes = pieces[0].shape[0]
    row, col = ids[0], ids[1]
    for k in range(n_row):
        gathered[place_of(row, k, n_row, nodes), :] = pieces[k][...]
    chunk = 2 * nodes
    for k in range(n_row // 2):
        lines = pl.ds(k * chunk, chunk)
        pre = dot(gathered[lines, :], weight[...]) + bias[...]
        hidden = (pre / (1.0 + jnp.exp(-pre))).astype(bf16)
        column_out[lines, :] = hidden
        high, low = halves(dot(hidden, class_weight[...], ((1,), (1,))))
        stacked[lines, :] = jnp.concatenate([high, low], axis=1)
    hidden_out[...] = column_out[place_of(row, 0, n_row, nodes), :]
    both = dot(dense[...], stacked[...])
    lanes = both.shape[1] // 2
    term = (both[:, :lanes] + both[:, lanes:]).T[: term_out.shape[0]]
    slice_of = lax.broadcasted_iota(jnp.int32, term.shape, 1) // nodes
    line = lax.broadcasted_iota(jnp.int32, term.shape, 0)
    codes = jnp.where(slice_of == col, jnp.concatenate([code[...]] * n_col, axis=1), 0.0)
    term_out[...] = jnp.where(line == term.shape[0] - 1, codes, term).astype(bf16)


def hidden_terms(ids, dense, weight, bias, class_weight, code, pieces, n_col, lines):
    nodes = pieces[0].shape[0]
    n_row = len(pieces)
    width = weight.shape[1]
    lanes = class_weight.shape[0]
    column = n_row * nodes
    return pl.pallas_call(
        functools.partial(hidden_kernel, n_row, n_col),
        out_shape=[
            jax.ShapeDtypeStruct((nodes, width), bf16),
            jax.ShapeDtypeStruct((column, width), bf16),
            jax.ShapeDtypeStruct((lines, n_col * nodes), bf16),
        ],
        in_specs=[SMEM] + [VMEM] * (5 + n_row),
        out_specs=[VMEM] * 3,
        scratch_shapes=[
            pltpu.VMEM((column, 2 * lanes), bf16),
            pltpu.VMEM((column, pieces[0].shape[1]), bf16),
        ],
        compiler_params=params(dense.size * 2 + column * width * 8 + 6 * MIB),
        cost_estimate=cost(4 * dense.size * lanes, dense.size * 2, column * width * 2),
        name="hidden_terms",
    )(ids, dense, weight, bias, class_weight, code, *pieces)


def slope_kernel(n_row, ids, weight, bias, *refs):
    pieces = refs[:n_row]
    slope_out, turned_out = refs[n_row:]
    nodes = pieces[0].shape[0]
    row = ids[0]
    for k in range(n_row):
        pre = dot(pieces[k][...], weight[...]) + bias[...]
        sigma = 1.0 / (1.0 + jnp.exp(-pre))
        place = place_of(row, k, n_row, nodes)
        slope_out[place, :] = sigma * (1.0 + pre * (1.0 - sigma))
        turned_out[:, place] = pieces[k][...].T


def slopes(ids, weight, bias, pieces):
    nodes, features = pieces[0].shape
    n_row = len(pieces)
    width = weight.shape[1]
    column = n_row * nodes
    return pl.pallas_call(
        functools.partial(slope_kernel, n_row),
        out_shape=[
            jax.ShapeDtypeStruct((column, width), f32),
            jax.ShapeDtypeStruct((features, column), bf16),
        ],
        in_specs=[SMEM] + [VMEM] * (2 + n_row),
        out_specs=[VMEM] * 2,
        compiler_params=params(column * width * 8 + 4 * MIB),
        cost_estimate=cost(2 * column * features * width, column * width * 4, column * width * 2),
        name="slopes",
    )(ids, weight, bias, *pieces)


def tree_sum(parts):
    parts = [part.astype(f32) for part in parts]
    while len(parts) > 1:
        parts = [parts[k] + parts[k + 1] for k in range(0, len(parts), 2)]
    return parts[0]


def gradient_kernel(n_col, classes, ids, dense, column, slope, turned, class_weight_turned, class_bias, *refs):
    terms = refs[:n_col]
    logits_out, keep_out, send_out, scratch, packed = refs[n_col:]
    lines, nodes_row = terms[0].shape
    nodes = nodes_row // n_col
    features = turned.shape[0]
    width = column.shape[1]
    row, col = ids[0], ids[1]
    total = tree_sum([term[...] for term in terms])
    code = total[lines - 1 :, :]
    live = (code >= MASK_CODE).astype(f32)
    label = (code - MASK_CODE * live).astype(jnp.int32)
    line = lax.broadcasted_iota(jnp.int32, total.shape, 0)
    bias = jnp.broadcast_to(class_bias[...], (8, class_bias.shape[1])).T[:lines, :1]
    logits = jnp.where(line < classes, total + bias, -jnp.inf)
    scratch[...] = logits
    own = pl.ds(pl.multiple_of(col * nodes, nodes), nodes)
    logits_out[...] = scratch[:classes, own]
    top = jnp.max(logits, axis=0, keepdims=True)
    log_total = top + jnp.log(jnp.sum(jnp.exp(logits - top), axis=0, keepdims=True))
    chosen = line == label
    picked = jnp.sum(jnp.where(chosen, logits, 0.0), axis=0, keepdims=True)
    grad = (jnp.exp(logits - log_total) - chosen.astype(f32)) * live
    high, low = halves(grad)
    stacked = jnp.concatenate([high, low], axis=0)
    both = dot(stacked, dense[...])
    back = both[:lines] + both[lines:]
    back_high, back_low = halves(back)
    back_both = jnp.concatenate([back_high, back_low], axis=0)
    class_both = dot(back_both, column[...])
    packed[pl.ds(features, lines), :] = class_both[:lines] + class_both[lines:]
    twice = jnp.concatenate([class_weight_turned[:lines, :]] * 2, axis=0)
    hidden_grad = dot(back_both, twice, ((0,), (0,)))
    pre_grad = hidden_grad * slope[...]
    packed[pl.ds(0, features), :] = dot(turned[...], pre_grad.astype(bf16))
    packed[pl.ds(features + lines - 1, 1), :] = jnp.sum(pre_grad, axis=0, keepdims=True)
    here = (lax.broadcasted_iota(jnp.int32, (8, nodes_row), 1) // nodes == col).astype(f32)
    ours = here.astype(bf16)
    class_sum = dot(ours, high, ((1,), (1,))) + dot(ours, low, ((1,), (1,)))
    class_sum = jnp.concatenate([class_sum, jnp.zeros((8, width - lines), f32)], axis=1)
    loss = jnp.sum((log_total - picked) * live * here[:1])
    members = jnp.sum(live * here[:1])
    lane = lax.broadcasted_iota(jnp.int32, (8, width), 1)
    entry = lax.broadcasted_iota(jnp.int32, (8, width), 0)
    loss = jnp.full((8, width), loss, f32)
    loss_high = loss.astype(bf16).astype(f32)
    loss_middle = (loss - loss_high).astype(bf16).astype(f32)
    loss_low = loss - loss_high - loss_middle
    values = jnp.where(entry == 0, loss_high, jnp.where(entry == 1, loss_middle, loss_low))
    values = jnp.where(entry == 3, members, jnp.where(entry < 3, values, 0.0))
    tail = jnp.where(lane == row * n_col + col, values, 0.0)
    packed[pl.ds(features + lines, 8), :] = class_sum
    packed[pl.ds(features + lines + 8, 8), :] = tail
    part = packed.shape[0] // 2
    core = row & 1
    keep_out[...] = packed[pl.ds(pl.multiple_of(core * part, 8), part), :].astype(keep_out.dtype)
    send_out[...] = packed[pl.ds(pl.multiple_of((1 - core) * part, 8), part), :].astype(send_out.dtype)


def gradients(ids, dense, column, slope, turned, class_weight_turned, class_bias, terms, classes):
    n_col = len(terms)
    lines, nodes_row = terms[0].shape
    width = column.shape[1]
    packed = turned.shape[0] + lines + 16
    return pl.pallas_call(
        functools.partial(gradient_kernel, n_col, classes),
        out_shape=[
            jax.ShapeDtypeStruct((classes, nodes_row // n_col), f32),
            jax.ShapeDtypeStruct((packed // 2, width), WIRE),
            jax.ShapeDtypeStruct((packed // 2, width), WIRE),
        ],
        in_specs=[SMEM] + [VMEM] * (6 + n_col),
        out_specs=[VMEM] * 3,
        scratch_shapes=[
            pltpu.VMEM((lines, nodes_row), f32),
            pltpu.VMEM((packed, width), f32),
        ],
        compiler_params=params(dense.size * 2 + column.size * 16 + 6 * MIB),
        cost_estimate=cost(4 * dense.size * lines, dense.size * 2),
        name="gradients",
    )(ids, dense, column, slope, turned, class_weight_turned, class_bias, *terms)


def finish_kernel(features, lines, classes, ids, mine, other, loss_out, weight_out, bias_out, class_out, class_bias_out, packed):
    part = mine.shape[0]
    core = ids[0] & 1
    packed[pl.ds(pl.multiple_of(core * part, 8), part), :] = mine[...].astype(f32)
    packed[pl.ds(pl.multiple_of((1 - core) * part, 8), part), :] = other[...].astype(f32)
    tail = packed[pl.ds(features + lines + 8, 8), :]
    sums = jnp.sum(tail, axis=1, keepdims=True)
    members = sums[3:4]
    loss_out[...] = (sums[0:1] + sums[1:2] + sums[2:3]) / members
    weight_out[...] = packed[pl.ds(0, features), :] / members
    bias_out[...] = packed[pl.ds(features + lines - 1, 1), :] / members
    class_out[...] = packed[pl.ds(features, classes), :] / members
    class_bias_out[...] = packed[pl.ds(features + lines, 1), :][:, :classes] / members


def finish(ids, mine, other, features, lines, classes):
    part, width = mine.shape
    return pl.pallas_call(
        functools.partial(finish_kernel, features, lines, classes),
        out_shape=[
            jax.ShapeDtypeStruct((1, 1), f32),
            jax.ShapeDtypeStruct((features, width), f32),
            jax.ShapeDtypeStruct((1, width), f32),
            jax.ShapeDtypeStruct((classes, width), f32),
            jax.ShapeDtypeStruct((1, classes), f32),
        ],
        in_specs=[SMEM, VMEM, VMEM],
        out_specs=[VMEM] * 5,
        scratch_shapes=[pltpu.VMEM((2 * part, width), f32)],
        compiler_params=params(4 * MIB),
        name="finish",
    )(ids, mine, other)


def swap(value, axis, mask):
    size = lax.axis_size(axis)
    return lax.ppermute(value, axis, [(k, k ^ mask) for k in range(size)])


def gather_row(value):
    size = lax.axis_size("row")
    even = [value] + [swap(value, "row", k) for k in range(2, size, 2)]
    odd = [swap(even[0], "row", 1)]
    odd += [swap(piece, "row", 1) for piece in even[1:]]
    return even, odd


def sum_over(value, axis, low, high):
    while low < high:
        step = min(2, high - low)
        parts = [value.astype(WIRE)]
        parts += [swap(parts[0], axis, k << low) for k in range(1, 1 << step)]
        value = tree_sum(parts)
        low += step
    return value


def step(
    node_features,
    tile_values,
    tile_rows,
    tile_cols,
    tile_count,
    labels,
    train_mask,
    hidden_weight,
    hidden_bias,
    class_weight,
    class_bias,
):
    nodes, features = node_features.shape
    classes = class_weight.shape[1]
    n_row, n_col = lax.axis_size("row"), lax.axis_size("col")
    row_bits, col_bits = n_row.bit_length() - 1, n_col.bit_length() - 1
    lines = (classes // 16 + 1) * 16
    ids = jnp.stack([lax.axis_index("row"), lax.axis_index("col")]).astype(jnp.int32)
    code = (labels + MASK_CODE * train_mask).astype(f32)[None, :]
    bias = hidden_bias[None, :]
    class_turned = jnp.pad(class_weight.T, ((0, TILE - classes), (0, 0)))
    class_bias_lanes = jnp.pad(class_bias, (0, TILE - classes))[None, :]

    near, far = gather_row(node_features)
    total = collect(
        tile_values[0, 0], tile_rows[0], tile_cols[0], tile_count, n_col * nodes // TILE, n_row * nodes // TILE
    )
    dense = round_block(total, n_col * nodes, n_row * nodes, n_row)
    terms = first_terms(ids, dense, [piece for pair in zip(near, far) for piece in pair], n_col)
    arrived = [terms[0]] + [swap(terms[k], "col", k) for k in range(1, n_col)]
    first_agg = tree_sum(arrived).astype(bf16)
    near, far = gather_row(first_agg)
    pieces = [piece for pair in zip(near, far) for piece in pair]
    hidden, column, term = hidden_terms(
        ids, dense, hidden_weight, bias, class_turned, code, pieces, n_col, lines
    )
    class_terms = [term] + [swap(term, "col", k) for k in range(1, n_col)]
    slope, turned = slopes(ids, hidden_weight, bias, pieces)
    logits, keep, send = gradients(
        ids, dense, column, slope, turned, class_turned, class_bias_lanes, class_terms, classes
    )
    part = keep.astype(f32) + swap(send, "row", 1).astype(f32)
    part = sum_over(part, "row", 1, row_bits)
    part = sum_over(part, "col", 0, col_bits)
    mine = part.astype(WIRE)
    other = swap(mine, "row", 1)
    loss, weight_grad, bias_grad, class_grad, class_bias_grad = finish(
        ids, mine, other, features, lines, classes
    )
    return (
        hidden,
        logits,
        loss[0, 0],
        weight_grad,
        bias_grad[0],
        class_grad.T,
        class_bias_grad[0],
    )


def solution(mesh):
    in_specs = (
        P(("row", "col"), None),
        P("row", "col", None, None, None),
        P("row", "col", None),
        P("row", "col", None),
        P("row", "col"),
        P(("row", "col")),
        P(("row", "col")),
        P(),
        P(),
        P(),
        P(),
    )
    out_specs = (P(("row", "col"), None), P(None, ("row", "col")), P(), P(), P(), P(), P())
    return jax.shard_map(step, mesh=mesh, in_specs=in_specs, out_specs=out_specs, check_vma=False)
```

```python
import functools
import math

import jax
import jax.numpy as jnp
from jax import lax
from jax.experimental import pallas as pl
from jax.experimental.pallas import tpu as pltpu
from jax.sharding import PartitionSpec as P


TILE = 128
MASK_CODE = 128
MIB = 1024 * 1024
WIRE = jnp.bfloat16
f32 = jnp.float32
bf16 = jnp.bfloat16


VMEM = pl.BlockSpec(memory_space=pltpu.VMEM)
SMEM = pl.BlockSpec(memory_space=pltpu.SMEM)
HBM = pl.BlockSpec(memory_space=pltpu.HBM)


def params(limit):
    return pltpu.CompilerParams(vmem_limit_bytes=limit)


def cost(flops, moved, transcendentals=0):
    return pl.CostEstimate(flops=flops, bytes_accessed=moved, transcendentals=transcendentals)


def dot(a, b, dims=((1,), (0,))):
    return lax.dot_general(a, b, (dims, ((), ())), preferred_element_type=f32)


def halves(value):
    high = value.astype(bf16)
    return high, (value - high.astype(f32)).astype(bf16)


def collect_kernel(group, depth, tile_cols, count, rows_hbm, cols_hbm, values, total, ring, rows, cols, sem, table_sem):
    slots = values.shape[0]
    groups = slots // group
    spare = total.shape[0] - 1
    tables = [
        pltpu.make_async_copy(source, target, table_sem.at[k])
        for k, (source, target) in enumerate(((rows_hbm, rows), (cols_hbm, cols)))
    ]
    for table in tables:
        table.start()

    def copy(index, slot):
        return pltpu.make_async_copy(
            values.at[pl.ds(index * group, group)], ring.at[slot], sem.at[slot]
        )

    live = count[0, 0]
    groups_live = (live + group - 1) // group
    for slot in range(depth):
        @pl.when(slot < groups_live)
        def _():
            copy(slot, slot).start()

    @pl.loop(0, spare // 4)
    def _(place):
        for k in range(4):
            total[place * 4 + k] = jnp.zeros((TILE, TILE), f32)

    for table in tables:
        table.wait()

    @pl.loop(0, groups_live)
    def _(index):
        slot = lax.rem(index, depth)
        copy(index, slot).wait()
        for k in range(group):
            item = index * group + k
            place = rows[0, item] * tile_cols + cols[0, item]
            place = jnp.where(item < live, place, spare)
            total[place] = total[place] + ring[slot, k].astype(f32)

        if depth < groups:
            @pl.when(index + depth < groups_live)
            def _():
                copy(index + depth, slot).start()


def collect(values, rows, cols, count, tile_rows, tile_cols):
    slots = values.shape[0]
    n_places = tile_rows * tile_cols
    group = math.gcd(slots, 16)
    small = n_places <= 128
    depth = slots // group if small else min(slots // group, 8)
    rows, cols = (pltpu.with_memory_space_constraint(x, pltpu.HBM) for x in (rows, cols))
    return pl.pallas_call(
        functools.partial(collect_kernel, group, depth, tile_cols),
        out_shape=jax.ShapeDtypeStruct((n_places + 1, TILE, TILE), f32),
        in_specs=[SMEM, HBM, HBM, HBM],
        out_specs=VMEM,
        scratch_shapes=[
            pltpu.VMEM((depth, group, TILE, TILE), bf16),
            pltpu.SMEM((1, slots), jnp.int32),
            pltpu.SMEM((1, slots), jnp.int32),
            pltpu.SemaphoreType.DMA((depth,)),
            pltpu.SemaphoreType.DMA((2,)),
        ],
        compiler_params=params((44 if small else 56) * MIB),
        cost_estimate=cost(slots * TILE * TILE, slots * TILE * TILE * 2),
        name="collect",
    )(count, rows, cols, values)


def position(row, k, n_row):
    other = row ^ k
    return (other & 1) * (n_row // 2) + (other >> 1)


def place_of(row, k, n_row, nodes):
    return pl.ds(pl.multiple_of(position(row, k, n_row) * nodes, nodes), nodes)


def round_kernel(n_row, total, dense):
    tile_rows = dense.shape[0] // TILE
    tile_cols = dense.shape[1] // TILE
    each = tile_cols // n_row

    @pl.loop(0, tile_rows)
    def _(tile_row):
        lines = pl.ds(pl.multiple_of(tile_row * TILE, TILE), TILE)
        for tile_col in range(tile_cols):
            target = position(tile_col // each, 0, n_row) * each + tile_col % each
            lanes = pl.ds(target * TILE, TILE)
            dense[lines, lanes] = total[tile_row * tile_cols + tile_col].astype(bf16)


def round_block(total, lines, columns, n_row):
    return pl.pallas_call(
        functools.partial(round_kernel, n_row),
        out_shape=jax.ShapeDtypeStruct((lines, columns), bf16),
        in_specs=[VMEM],
        out_specs=VMEM,
        compiler_params=params(lines * columns * 6 + 6 * MIB),
        cost_estimate=cost(lines * columns, lines * columns * 6),
        name="round_block",
    )(total)


def first_kernel(n_row, n_col, ids, dense, *refs):
    pieces, outs = refs[:n_row], refs[n_row : n_row + n_col]
    stacked, whole = refs[-2:]
    nodes = pieces[0].shape[0]
    row, col = ids[0], ids[1]
    for k in range(n_row):
        stacked[place_of(row, k, n_row, nodes), :] = pieces[k][...]
    whole[...] = dot(dense[...], stacked[...]).astype(bf16)
    for k in range(n_col):
        outs[k][...] = whole[pl.ds(pl.multiple_of((col ^ k) * nodes, nodes), nodes), :]


def first_terms(ids, dense, pieces, n_col):
    nodes, width = pieces[0].shape
    n_row = len(pieces)
    return pl.pallas_call(
        functools.partial(first_kernel, n_row, n_col),
        out_shape=[jax.ShapeDtypeStruct((nodes, width), bf16)] * n_col,
        in_specs=[SMEM, VMEM] + [VMEM] * n_row,
        out_specs=[VMEM] * n_col,
        scratch_shapes=[
            pltpu.VMEM((n_row * nodes, width), bf16),
            pltpu.VMEM((n_col * nodes, width), bf16),
        ],
        compiler_params=params(dense.size * 2 + 6 * MIB),
        cost_estimate=cost(2 * dense.size * width, dense.size * 2),
        name="first_terms",
    )(ids, dense, *pieces)


def hidden_kernel(n_row, n_col, ids, dense, weight, bias, class_weight, code, *refs):
    pieces = refs[:n_row]
    hidden_out, column_out, term_out, stacked, gathered = refs[n_row:]
    nodes = pieces[0].shape[0]
    row, col = ids[0], ids[1]
    for k in range(n_row):
        gathered[place_of(row, k, n_row, nodes), :] = pieces[k][...]
    chunk = 2 * nodes
    for k in range(n_row // 2):
        lines = pl.ds(k * chunk, chunk)
        pre = dot(gathered[lines, :], weight[...]) + bias[...]
        hidden = (pre / (1.0 + jnp.exp(-pre))).astype(bf16)
        column_out[lines, :] = hidden
        high, low = halves(dot(hidden, class_weight[...], ((1,), (1,))))
        stacked[lines, :] = jnp.concatenate([high, low], axis=1)
    hidden_out[...] = column_out[place_of(row, 0, n_row, nodes), :]
    both = dot(dense[...], stacked[...])
    lanes = both.shape[1] // 2
    term = (both[:, :lanes] + both[:, lanes:]).T[: term_out.shape[0]]
    slice_of = lax.broadcasted_iota(jnp.int32, term.shape, 1) // nodes
    line = lax.broadcasted_iota(jnp.int32, term.shape, 0)
    codes = jnp.where(slice_of == col, jnp.concatenate([code[...]] * n_col, axis=1), 0.0)
    term_out[...] = jnp.where(line == term.shape[0] - 1, codes, term).astype(bf16)


def hidden_terms(ids, dense, weight, bias, class_weight, code, pieces, n_col, lines):
    nodes = pieces[0].shape[0]
    n_row = len(pieces)
    width = weight.shape[1]
    lanes = class_weight.shape[0]
    column = n_row * nodes
    return pl.pallas_call(
        functools.partial(hidden_kernel, n_row, n_col),
        out_shape=[
            jax.ShapeDtypeStruct((nodes, width), bf16),
            jax.ShapeDtypeStruct((column, width), bf16),
            jax.ShapeDtypeStruct((lines, n_col * nodes), bf16),
        ],
        in_specs=[SMEM] + [VMEM] * (5 + n_row),
        out_specs=[VMEM] * 3,
        scratch_shapes=[
            pltpu.VMEM((column, 2 * lanes), bf16),
            pltpu.VMEM((column, pieces[0].shape[1]), bf16),
        ],
        compiler_params=params(dense.size * 2 + column * width * 8 + 6 * MIB),
        cost_estimate=cost(4 * dense.size * lanes, dense.size * 2, column * width * 2),
        name="hidden_terms",
    )(ids, dense, weight, bias, class_weight, code, *pieces)


def slope_kernel(n_row, ids, weight, bias, *refs):
    pieces = refs[:n_row]
    slope_out, turned_out = refs[n_row:]
    nodes = pieces[0].shape[0]
    row = ids[0]
    for k in range(n_row):
        pre = dot(pieces[k][...], weight[...]) + bias[...]
        sigma = 1.0 / (1.0 + jnp.exp(-pre))
        place = place_of(row, k, n_row, nodes)
        slope_out[place, :] = sigma * (1.0 + pre * (1.0 - sigma))
        turned_out[:, place] = pieces[k][...].T


def slopes(ids, weight, bias, pieces):
    nodes, features = pieces[0].shape
    n_row = len(pieces)
    width = weight.shape[1]
    column = n_row * nodes
    return pl.pallas_call(
        functools.partial(slope_kernel, n_row),
        out_shape=[
            jax.ShapeDtypeStruct((column, width), f32),
            jax.ShapeDtypeStruct((features, column), bf16),
        ],
        in_specs=[SMEM] + [VMEM] * (2 + n_row),
        out_specs=[VMEM] * 2,
        compiler_params=params(column * width * 8 + 4 * MIB),
        cost_estimate=cost(2 * column * features * width, column * width * 4, column * width * 2),
        name="slopes",
    )(ids, weight, bias, *pieces)


def tree_sum(parts):
    parts = [part.astype(f32) for part in parts]
    while len(parts) > 1:
        parts = [parts[k] + parts[k + 1] for k in range(0, len(parts), 2)]
    return parts[0]


def gradient_kernel(n_col, classes, ids, dense, column, slope, turned, class_weight_turned, class_bias, *refs):
    terms = refs[:n_col]
    logits_out, keep_out, send_out, scratch, packed = refs[n_col:]
    lines, nodes_row = terms[0].shape
    nodes = nodes_row // n_col
    features = turned.shape[0]
    width = column.shape[1]
    row, col = ids[0], ids[1]
    total = tree_sum([term[...] for term in terms])
    code = total[lines - 1 :, :]
    live = (code >= MASK_CODE).astype(f32)
    label = (code - MASK_CODE * live).astype(jnp.int32)
    line = lax.broadcasted_iota(jnp.int32, total.shape, 0)
    bias = jnp.broadcast_to(class_bias[...], (8, class_bias.shape[1])).T[:lines, :1]
    logits = jnp.where(line < classes, total + bias, -jnp.inf)
    scratch[...] = logits
    own = pl.ds(pl.multiple_of(col * nodes, nodes), nodes)
    logits_out[...] = scratch[:classes, own]
    top = jnp.max(logits, axis=0, keepdims=True)
    log_total = top + jnp.log(jnp.sum(jnp.exp(logits - top), axis=0, keepdims=True))
    chosen = line == label
    picked = jnp.sum(jnp.where(chosen, logits, 0.0), axis=0, keepdims=True)
    grad = (jnp.exp(logits - log_total) - chosen.astype(f32)) * live
    high, low = halves(grad)
    stacked = jnp.concatenate([high, low], axis=0)
    both = dot(stacked, dense[...])
    back = both[:lines] + both[lines:]
    back_high, back_low = halves(back)
    back_both = jnp.concatenate([back_high, back_low], axis=0)
    class_both = dot(back_both, column[...])
    packed[pl.ds(features, lines), :] = class_both[:lines] + class_both[lines:]
    twice = jnp.concatenate([class_weight_turned[:lines, :]] * 2, axis=0)
    chunk = 2 * nodes
    weight_grad = jnp.zeros((features, width), f32)
    bias_grad = jnp.zeros((1, width), f32)
    for k in range(column.shape[0] // chunk):
        first, last = k * chunk, (k + 1) * chunk
        hidden_grad = dot(back_both[:, first:last], twice, ((0,), (0,)))
        pre_grad = hidden_grad * slope[first:last, :]
        weight_grad += dot(turned[:, first:last], pre_grad.astype(bf16))
        bias_grad += jnp.sum(pre_grad, axis=0, keepdims=True)
    packed[pl.ds(0, features), :] = weight_grad
    packed[pl.ds(features + lines - 1, 1), :] = bias_grad
    here = (lax.broadcasted_iota(jnp.int32, (8, nodes_row), 1) // nodes == col).astype(f32)
    ours = here.astype(bf16)
    class_sum = dot(ours, high, ((1,), (1,))) + dot(ours, low, ((1,), (1,)))
    class_sum = jnp.concatenate([class_sum, jnp.zeros((8, width - lines), f32)], axis=1)
    loss = jnp.sum((log_total - picked) * live * here[:1])
    members = jnp.sum(live * here[:1])
    lane = lax.broadcasted_iota(jnp.int32, (8, width), 1)
    entry = lax.broadcasted_iota(jnp.int32, (8, width), 0)
    loss = jnp.full((8, width), loss, f32)
    loss_high = loss.astype(bf16).astype(f32)
    loss_middle = (loss - loss_high).astype(bf16).astype(f32)
    loss_low = loss - loss_high - loss_middle
    values = jnp.where(entry == 0, loss_high, jnp.where(entry == 1, loss_middle, loss_low))
    values = jnp.where(entry == 3, members, jnp.where(entry < 3, values, 0.0))
    tail = jnp.where(lane == row * n_col + col, values, 0.0)
    packed[pl.ds(features + lines, 8), :] = class_sum
    packed[pl.ds(features + lines + 8, 8), :] = tail
    part = packed.shape[0] // 2
    core = row & 1
    keep_out[...] = packed[pl.ds(pl.multiple_of(core * part, 8), part), :].astype(keep_out.dtype)
    send_out[...] = packed[pl.ds(pl.multiple_of((1 - core) * part, 8), part), :].astype(send_out.dtype)


def gradients(ids, dense, column, slope, turned, class_weight_turned, class_bias, terms, classes):
    n_col = len(terms)
    lines, nodes_row = terms[0].shape
    width = column.shape[1]
    packed = turned.shape[0] + lines + 16
    return pl.pallas_call(
        functools.partial(gradient_kernel, n_col, classes),
        out_shape=[
            jax.ShapeDtypeStruct((classes, nodes_row // n_col), f32),
            jax.ShapeDtypeStruct((packed // 2, width), WIRE),
            jax.ShapeDtypeStruct((packed // 2, width), WIRE),
        ],
        in_specs=[SMEM] + [VMEM] * (6 + n_col),
        out_specs=[VMEM] * 3,
        scratch_shapes=[
            pltpu.VMEM((lines, nodes_row), f32),
            pltpu.VMEM((packed, width), f32),
        ],
        compiler_params=params(dense.size * 2 + column.size * 16 + 6 * MIB),
        cost_estimate=cost(4 * dense.size * lines, dense.size * 2),
        name="gradients",
    )(ids, dense, column, slope, turned, class_weight_turned, class_bias, *terms)


def finish_kernel(features, lines, classes, ids, mine, other, loss_out, weight_out, bias_out, class_out, class_bias_out, packed):
    part = mine.shape[0]
    core = ids[0] & 1
    packed[pl.ds(pl.multiple_of(core * part, 8), part), :] = mine[...].astype(f32)
    packed[pl.ds(pl.multiple_of((1 - core) * part, 8), part), :] = other[...].astype(f32)
    tail = packed[pl.ds(features + lines + 8, 8), :]
    sums = jnp.sum(tail, axis=1, keepdims=True)
    members = sums[3:4]
    loss_out[...] = (sums[0:1] + sums[1:2] + sums[2:3]) / members
    weight_out[...] = packed[pl.ds(0, features), :] / members
    bias_out[...] = packed[pl.ds(features + lines - 1, 1), :] / members
    class_out[...] = packed[pl.ds(features, classes), :] / members
    class_bias_out[...] = packed[pl.ds(features + lines, 1), :][:, :classes] / members


def finish(ids, mine, other, features, lines, classes):
    part, width = mine.shape
    return pl.pallas_call(
        functools.partial(finish_kernel, features, lines, classes),
        out_shape=[
            jax.ShapeDtypeStruct((1, 1), f32),
            jax.ShapeDtypeStruct((features, width), f32),
            jax.ShapeDtypeStruct((1, width), f32),
            jax.ShapeDtypeStruct((classes, width), f32),
            jax.ShapeDtypeStruct((1, classes), f32),
        ],
        in_specs=[SMEM, VMEM, VMEM],
        out_specs=[VMEM] * 5,
        scratch_shapes=[pltpu.VMEM((2 * part, width), f32)],
        compiler_params=params(4 * MIB),
        name="finish",
    )(ids, mine, other)


def swap(value, axis, mask):
    size = lax.axis_size(axis)
    return lax.ppermute(value, axis, [(k, k ^ mask) for k in range(size)])


def gather_row(value):
    size = lax.axis_size("row")
    even = [value] + [swap(value, "row", k) for k in range(2, size, 2)]
    odd = [swap(even[0], "row", 1)]
    odd += [swap(piece, "row", 1) for piece in even[1:]]
    return even, odd


def sum_over(value, axis, low, high):
    while low < high:
        step = min(2, high - low)
        parts = [value.astype(WIRE)]
        parts += [swap(parts[0], axis, k << low) for k in range(1, 1 << step)]
        value = tree_sum(parts)
        low += step
    return value


def step(
    node_features,
    tile_values,
    tile_rows,
    tile_cols,
    tile_count,
    labels,
    train_mask,
    hidden_weight,
    hidden_bias,
    class_weight,
    class_bias,
):
    nodes, features = node_features.shape
    classes = class_weight.shape[1]
    n_row, n_col = lax.axis_size("row"), lax.axis_size("col")
    row_bits, col_bits = n_row.bit_length() - 1, n_col.bit_length() - 1
    lines = (classes // 16 + 1) * 16
    ids = jnp.stack([lax.axis_index("row"), lax.axis_index("col")]).astype(jnp.int32)
    code = (labels + MASK_CODE * train_mask).astype(f32)[None, :]
    bias = hidden_bias[None, :]
    class_turned = jnp.pad(class_weight.T, ((0, TILE - classes), (0, 0)))
    class_bias_lanes = jnp.pad(class_bias, (0, TILE - classes))[None, :]

    near, far = gather_row(node_features)
    total = collect(
        tile_values[0, 0], tile_rows[0], tile_cols[0], tile_count, n_col * nodes // TILE, n_row * nodes // TILE
    )
    dense = round_block(total, n_col * nodes, n_row * nodes, n_row)
    terms = first_terms(ids, dense, [piece for pair in zip(near, far) for piece in pair], n_col)
    arrived = [terms[0]] + [swap(terms[k], "col", k) for k in range(1, n_col)]
    first_agg = tree_sum(arrived).astype(bf16)
    near, far = gather_row(first_agg)
    pieces = [piece for pair in zip(near, far) for piece in pair]
    hidden, column, term = hidden_terms(
        ids, dense, hidden_weight, bias, class_turned, code, pieces, n_col, lines
    )
    class_terms = [term] + [swap(term, "col", k) for k in range(1, n_col)]
    slope, turned = slopes(ids, hidden_weight, bias, pieces)
    logits, keep, send = gradients(
        ids, dense, column, slope, turned, class_turned, class_bias_lanes, class_terms, classes
    )
    part = keep.astype(f32) + swap(send, "row", 1).astype(f32)
    part = sum_over(part, "row", 1, row_bits)
    part = sum_over(part, "col", 0, col_bits)
    mine = part.astype(WIRE)
    other = swap(mine, "row", 1)
    loss, weight_grad, bias_grad, class_grad, class_bias_grad = finish(
        ids, mine, other, features, lines, classes
    )
    return (
        hidden,
        logits,
        loss[0, 0],
        weight_grad,
        bias_grad[0],
        class_grad.T,
        class_bias_grad[0],
    )


def solution(mesh):
    in_specs = (
        P(("row", "col"), None),
        P("row", "col", None, None, None),
        P("row", "col", None),
        P("row", "col", None),
        P("row", "col"),
        P(("row", "col")),
        P(("row", "col")),
        P(),
        P(),
        P(),
        P(),
    )
    out_specs = (P(("row", "col"), None), P(None, ("row", "col")), P(), P(), P(), P(), P())
    return jax.shard_map(step, mesh=mesh, in_specs=in_specs, out_specs=out_specs, check_vma=False)
```
